256 devices in a mesh: nodes: 64 (over x, z, core), feat: 4 (over y).
Axes of the slice: x: 4, y: 4, z: 8, core: 2. Of those that a mesh axis runs over, the one named last changes fastest.
Arguments:
- node_feats: bfloat16 [32768, 512], P('nodes', 'feat'), may hold values from -6 to 6
- weight_one: bfloat16 [512, 512], replicated, may hold values from -0.25 to 0.25
- weight_two: bfloat16 [512, 512], replicated, may hold values from -0.25 to 0.25
- adj_tiles: bfloat16 [256, 24, 128, 128], P('nodes'), may hold values from -0.109375 to 0.109375
- tile_owner: int32 [6144, 1], P('nodes'), may hold values from 0 to 63; in each aligned block of 96 rows (0 to 95, 96 to 191, ...) at most 2 rows name the same one
- tile_local: int32 [6144, 1], P('nodes'), may hold values from 0 to 3
- cotangent: bfloat16 [32768, 512], P('nodes', 'feat'), may hold values from -6 to 6
Outputs:
- layer_output: bfloat16 [32768, 512], P('nodes', 'feat')
- grad_one: float32 [512, 512], P('feat')
- grad_two: float32 [512, 512], P('feat')
The draws below stay inside these ranges and needn't reach their ends.
Inputs may be any that keep to these rules, and one draw needn't show every extreme that they name: `tile_owner`: among the 96 tiles of one index of nodes, each owner index is named by at most 2 tiles, and exactly 2 for some owner.
All inputs are finite; a program needn't handle non-finite values.
Results may differ from the reference program's by a relative error of at most 0.0065.
Values may be sent and summed in bfloat16 or wider, within the bound.
No kernel may reach another device: no remote copies, remote signals or barrier semaphores. Data moves between devices by JAX's collectives and lax.ppermute only.
A program may use at most 128 MiB of HBM per device.

```python
import math
import jax
import jax.numpy as jnp
import numpy as np
from jax import lax

F = 512
BLK = 128
NB = 4
K = 24
NBLK = 256
NODES = 32768
TILES = 6144
CAP = 2
N_NODES = 64


def with_ends(array, key, least, high):
    longest = array.shape.index(max(array.shape))
    spots = []
    for shift in (0, 1):
        where = [jax.random.randint(jax.random.fold_in(key, axis), (), 0, length) for axis, length in enumerate(array.shape)]
        where[longest] = (where[longest] + shift) % array.shape[longest]
        spots.append(tuple(where))
    return array.at[spots[0]].set(least).at[spots[1]].set(high)


def shard_levels(rng, shape, shards, smallest, high):
    loudness = 1.0
    for axis_at, parts in shards:
        steps = jax.random.uniform(jax.random.fold_in(jax.random.fold_in(rng, 6), axis_at), (parts,), jnp.float32, smallest / len(shards), high / len(shards))
        loudness = loudness * jnp.repeat(jnp.exp(steps), shape[axis_at] // parts).reshape((-1,) + (1,) * (len(shape) - 1 - axis_at))
    return loudness


def shared_out(key, own, number, rows, amount, top, reach, slope):
    sequence = jax.random.permutation(key, amount)
    crowded, usual = shares(amount, rows * top, reach, slope, True), shares(amount, rows * top, reach, slope, False)
    places = jnp.arange(amount)

    def named(sizes, turn):
        used = int((sizes > 0).sum())
        fixed = max(1, used // 4)
        moved = fixed + (places - fixed + turn * (used - fixed)) % max(1, amount - fixed)
        return jnp.zeros((amount,), jnp.int32).at[sequence[jnp.where(places < fixed, places, moved)]].set(jnp.asarray(sizes, jnp.int32))

    sizes = jnp.where(number % 4 == 0, named(crowded, number // 4), named(usual, number - number // 4 - 1))
    mixed = jax.random.permutation(jax.random.fold_in(own, 3), amount)
    giver, taker = mixed[0:amount // 2 * 2:2], mixed[1:amount // 2 * 2:2]
    margin = jnp.minimum(sizes[giver] - 1, reach - sizes[taker]) // 2
    margin = jnp.where((giver == sequence[0]) | (taker == sequence[0]) | (sizes[taker] == 0), 0, jnp.maximum(margin, 0))
    moved = jax.random.randint(jax.random.fold_in(own, 4), (amount // 2,), 0, 1 << 20) % (margin + 1)
    sizes = sizes.at[giver].add(-moved).at[taker].add(moved)
    labels = jnp.searchsorted(jnp.cumsum(sizes), jnp.arange(rows * top), side="right").astype(jnp.int32)
    grid = labels.reshape(top, rows).T
    grid = grid[jax.random.permutation(jax.random.fold_in(own, 1), rows)]
    turn = jax.random.randint(jax.random.fold_in(own, 2), (rows, 1), 0, top)
    return jnp.take_along_axis(grid, (jnp.arange(top)[None, :] + turn) % top, axis=1)


def shares(amount, total, most, skew, full):
    portions = [(1 << 20) // math.isqrt(rank ** skew) + 1 for rank in range(1, amount + 1)]
    largest = most if full else min(most, max(-(-total // amount), total * portions[0] // sum(portions)))
    least = 1 if total - largest >= amount - 1 else 0
    holding, rest = [largest] + [least] * (amount - 1), total - largest - least * (amount - 1)
    while rest > 0:
        movable = [i for i in range(1, amount) if holding[i] < largest] or [i for i in range(1, amount) if holding[i] < most]
        pool, left = sum([portions[i] for i in movable]), rest
        for i in movable:
            addition = min(most - holding[i], max(1, left * portions[i] // pool), rest)
            holding[i] = holding[i] + addition
            rest = rest - addition
    return np.array(holding)


def bell_draw(key, dims, spread, limit, shards=(), dtype=jnp.bfloat16):
    array = jax.random.normal(key, dims, jnp.float32) * spread
    if len(shards) > 0:
        array = shard_levels(key, dims, shards, -0.22, 0.18) * array
    return jnp.clip(array, min=-limit, max=limit).astype(dtype)


def setup_inputs(seed: int = 0) -> dict:
    streams_of = jax.random.split(jax.random.key(seed), 8)
    node_feats = bell_draw(streams_of[0], (NODES, F), 1.0, 6.0, ((0, 64), (1, 4)))
    weight_one = bell_draw(streams_of[1], (F, F), F ** -0.5, 0.25)
    weight_two = bell_draw(streams_of[2], (F, F), F ** -0.5, 0.25)
    adj_tiles = bell_draw(streams_of[3], (NBLK, K, BLK, BLK), (K * BLK) ** -0.5, 0.109375, ((0, 64),))
    tile_owner_keys = jax.random.split(jax.random.fold_in(streams_of[4], 1), TILES // (NB * K))
    tile_owner_turns = jax.random.permutation(jax.random.fold_in(streams_of[4], 3), TILES // (NB * K))
    tile_owner = jax.vmap(lambda own, number: shared_out(jax.random.fold_in(streams_of[4], 2), own, number, NB * K, N_NODES, 1, CAP, 2))(tile_owner_keys, tile_owner_turns).reshape((TILES, 1))
    tile_local = with_ends(jax.random.randint(streams_of[5], (TILES, 1), 0, NB), jax.random.fold_in(streams_of[5], 1), 0, NB - 1).astype(jnp.int32)
    cotangent = bell_draw(streams_of[6], (NODES, F), 1.0, 6.0, ((0, 64), (1, 4)))
    return {"node_feats": node_feats, "weight_one": weight_one, "weight_two": weight_two, "adj_tiles": adj_tiles, "tile_owner": tile_owner, "tile_local": tile_local, "cotangent": cotangent}


def propagate(adj_tiles, columns, features):
    blocks = features.reshape(NBLK, BLK, -1)

    def one_row(pieces):
        tile_row, column_row = pieces
        picked = blocks[column_row].astype(jnp.float32)
        return jnp.einsum('kij,kjf->if', tile_row.astype(jnp.float32), picked)
    summed = lax.map(one_row, (adj_tiles, columns))
    return summed.reshape(NODES, -1)

def transpose_sum(adj_tiles, columns, grads):
    blocks = grads.reshape(NBLK, BLK, -1).astype(jnp.float32)

    def one_step(total, pieces):
        tile_row, column_row, grad_block = pieces
        terms = jnp.einsum('kji,jf->kif', tile_row.astype(jnp.float32), grad_block)
        return (total.at[column_row].add(terms), None)
    start = jnp.zeros((NBLK, BLK, grads.shape[1]), jnp.float32)
    total, unused = lax.scan(one_step, start, (adj_tiles, columns, blocks))
    return total.reshape(NODES, -1)

def reference(node_feats, weight_one, weight_two, adj_tiles, tile_owner, tile_local, cotangent):
    columns = (tile_owner[:, 0] * NB + tile_local[:, 0]).astype(jnp.int32).reshape(NBLK, K)
    prop_one = propagate(adj_tiles, columns, node_feats).astype(jnp.bfloat16)
    z_one = jnp.dot(prop_one, weight_one, preferred_element_type=jnp.float32)
    hidden = (z_one * jax.nn.sigmoid(z_one)).astype(jnp.bfloat16)
    prop_two = propagate(adj_tiles, columns, hidden).astype(jnp.bfloat16)
    layer_output = jnp.dot(prop_two, weight_two, preferred_element_type=jnp.float32).astype(jnp.bfloat16)
    factor = 1.0 / math.sqrt(NODES)
    grad_two = jnp.dot(prop_two.T, cotangent, preferred_element_type=jnp.float32) * factor
    grad_prop = jnp.dot(cotangent, weight_two.T, preferred_element_type=jnp.float32).astype(jnp.bfloat16)
    grad_hidden = transpose_sum(adj_tiles, columns, grad_prop)
    sigma = jax.nn.sigmoid(z_one)
    grad_z = (grad_hidden * sigma * (1.0 + z_one * (1.0 - sigma))).astype(jnp.bfloat16)
    grad_one = jnp.dot(prop_one.T, grad_z, preferred_element_type=jnp.float32) * factor
    return (layer_output, grad_one, grad_two)
```

```python
import math

import jax
import jax.numpy as jnp
from jax import lax
from jax.experimental import pallas as pl
from jax.experimental.pallas import tpu as pltpu
from jax.sharding import PartitionSpec as P


NX, NZ, NC, NY = 4, 8, 2, 4


def node_pairs(dx, dz, dc):
    pairs = []
    for x in range(NX):
        for z in range(NZ):
            for c in range(NC):
                there = (((x + dx) % NX) * NZ + (z + dz) % NZ) * NC + (c + dc) % NC
                pairs.append(((x * NZ + z) * NC + c, there))
    return pairs


def xor_pairs(bit):
    return [(i, i ^ bit) for i in range(NX * NZ * NC)]


def send(value, dx=0, dz=0, dc=0):
    return lax.ppermute(value, "nodes", node_pairs(dx, dz, dc))


def send_y(value, dy):
    return lax.ppermute(value, "feat", [(y, (y + dy) % NY) for y in range(NY)])


def gather_y(value):
    return [value] + [send_y(value, -r) for r in range(1, NY)]


def join(parts):
    return parts[0] if len(parts) == 1 else jnp.concatenate(parts, axis=0)


def ring_z(block):
    half = block.shape[0] // 2
    low, high = [block], [block]
    for _ in range(3):
        low.append(send(low[-1], dz=1))
        high.append(send(high[-1], dz=-1))
    first = send(low[3][:half], dz=1)
    second = send(high[3][half:], dz=-1)
    return [[block], [high[1]], [high[2]], [high[3]], [first, second], [low[3]], [low[2]], [low[1]]]


def gather_plane(own):
    nb = own.shape[0]
    beside = [send(own, dx=-r) for r in (1, 2, 3)]
    others = join(beside)
    pieces = []
    for r, parts in enumerate(ring_z(own)):
        at = r * NX * nb
        for part in parts:
            pieces.append((at, part))
            at += part.shape[0]
    for r, parts in enumerate(ring_z(others)):
        at = r * NX * nb + nb
        for part in parts:
            pieces.append((at, part))
            at += part.shape[0]
    return pieces


def add16(a, b):
    return (a.astype(jnp.float32) + b.astype(jnp.float32)).astype(jnp.bfloat16)


def reduce_plane(parts, nb):
    half = NZ * nb // 2
    far = parts[2]
    up_far = send(far[:half], dx=1)
    down_far = send(far[half:], dx=-1)
    up_plain = send(parts[1][half:], dx=1)
    down_plain = send(parts[3][:half], dx=-1)
    up_sum = send(add16(parts[1][:half], up_far), dx=1)
    down_sum = send(add16(parts[3][half:], down_far), dx=-1)
    f32 = jnp.float32
    low = parts[0][:half].astype(f32) + up_sum.astype(f32) + down_plain.astype(f32)
    high = parts[0][half:].astype(f32) + up_plain.astype(f32) + down_sum.astype(f32)
    rows = [low[r * nb:(r + 1) * nb] for r in range(NZ // 2)] + [high[r * nb:(r + 1) * nb] for r in range(NZ // 2)]
    cut = nb // 2
    bf = jnp.bfloat16
    up = send(rows[4][:cut].astype(bf), dz=1)
    down = send(rows[4][cut:].astype(bf), dz=-1)
    up = jnp.concatenate([(rows[3][:cut] + up.astype(f32)), rows[3][cut:]], axis=0).astype(bf)
    down = jnp.concatenate([rows[5][:cut], rows[5][cut:] + down.astype(f32)], axis=0).astype(bf)
    for r in (2, 1):
        up = (rows[r] + send(up, dz=1).astype(f32)).astype(bf)
        down = (rows[8 - r] + send(down, dz=-1).astype(f32)).astype(bf)
    return rows[0] + send(up, dz=1).astype(f32) + send(down, dz=-1).astype(f32)


def all_reduce(value, index):
    cuts = []
    bits = (1, 16, 32, 2, 4, 8)
    for bit in bits:
        half = value.shape[0] // 2
        upper = (index & bit) != 0
        mine = jnp.where(upper, value[half:], value[:half])
        give = jnp.where(upper, value[:half], value[half:])
        value = mine + lax.ppermute(give, "nodes", xor_pairs(bit))
        cuts.append(upper)
    for bit, upper in zip(reversed(bits), reversed(cuts)):
        other = lax.ppermute(value, "nodes", xor_pairs(bit))
        value = jnp.concatenate([jnp.where(upper, other, value), jnp.where(upper, value, other)], axis=0)
    return value


def transposed_kernel(slot_a, slot_b, tiles_a, tiles_b, cot_a, cot_b, out_0, out_1, out_2, out_3, acc):
    count = tiles_a.shape[0]
    blk = tiles_a.shape[1]
    rows = cot_a.shape[0] // blk
    per = count // rows
    acc[...] = jnp.zeros_like(acc)
    for slots, tiles, cot in ((slot_a, tiles_a, cot_a), (slot_b, tiles_b, cot_b)):
        for b in range(rows):
            turned = cot[b * blk:(b + 1) * blk, :].T

            def one(i, carry, slots=slots, tiles=tiles, turned=turned, b=b):
                for j in range(4):
                    k = b * per + i * 4 + j
                    term = jnp.dot(turned, tiles[k], preferred_element_type=jnp.float32)
                    at = slots[k]
                    acc[at] = acc[at] + term
                return carry

            lax.fori_loop(0, per // 4, one, 0)
    size = out_0.shape[0]
    for r, out in enumerate((out_0, out_1, out_2, out_3)):
        out[...] = acc[r * size:(r + 1) * size].astype(out.dtype)


def transposed_terms(slots_a, slots_b, tiles_a, tiles_b, cot_a, cot_b, total):
    blk = tiles_a.shape[1]
    width = cot_a.shape[1]
    shape = jax.ShapeDtypeStruct((total // NX, width, blk), jnp.bfloat16)
    smem = pl.BlockSpec(memory_space=pltpu.SMEM)
    vmem = pl.BlockSpec(memory_space=pltpu.VMEM)
    return pl.pallas_call(
        transposed_kernel,
        out_shape=[shape] * NX,
        in_specs=[smem, smem, vmem, vmem, vmem, vmem],
        out_specs=[vmem] * NX,
        scratch_shapes=[pltpu.VMEM((total + 1, width, blk), jnp.float32)],
        compiler_params=pltpu.CompilerParams(vmem_limit_bytes=48 * 1024 * 1024),
        name="transposed_terms",
    )(slots_a, slots_b, tiles_a, tiles_b, cot_a, cot_b)


def spread_call(slots_a, slots_b, tiles_a, tiles_b, pieces, total, rows):
    count, blk, _ = tiles_a.shape
    width = pieces[0][1].shape[2]
    per = count // rows
    n = len(pieces)
    starts = [at for at, _ in pieces]
    sizes = [part.shape[0] for _, part in pieces]

    def kernel(slot_a, slot_b, tiles_a, tiles_b, *rest):
        parts, (out_a, out_b, held, sems) = rest[:n], rest[n:]
        copies = [
            pltpu.make_async_copy(part, held.at[pl.ds(at, size)], sems.at[i])
            for i, (part, at, size) in enumerate(zip(parts, starts, sizes))
        ]
        for copy in copies:
            copy.start()
        held[total] = jnp.zeros_like(held[total])
        for copy in copies:
            copy.wait()
        for slots, tiles, out in ((slot_a, tiles_a, out_a), (slot_b, tiles_b, out_b)):
            for b in range(rows):

                def one(i, summed, slots=slots, tiles=tiles, b=b):
                    for j in range(3):
                        k = b * per + i * 6 + j * 2
                        left = jnp.concatenate([tiles[k], tiles[k + 1]], axis=1)
                        right = jnp.concatenate([held[slots[k]], held[slots[k + 1]]], axis=0)
                        summed = summed + jnp.dot(left, right, preferred_element_type=jnp.float32)
                    return summed

                zero = jnp.zeros((blk, width), jnp.float32)
                out[b] = lax.fori_loop(0, per // 6, one, zero)

    shape = jax.ShapeDtypeStruct((rows, blk, width), jnp.float32)
    smem = pl.BlockSpec(memory_space=pltpu.SMEM)
    vmem = pl.BlockSpec(memory_space=pltpu.VMEM)
    return pl.pallas_call(
        kernel,
        out_shape=[shape, shape],
        in_specs=[smem, smem, vmem, vmem] + [pl.BlockSpec(memory_space=pl.ANY)] * n,
        out_specs=[vmem, vmem],
        scratch_shapes=[
            pltpu.VMEM((total + 1, blk, width), jnp.bfloat16),
            pltpu.SemaphoreType.DMA((n,)),
        ],
        compiler_params=pltpu.CompilerParams(vmem_limit_bytes=40 * 1024 * 1024),
        name="spread",
    )(slots_a, slots_b, tiles_a, tiles_b, *[part for _, part in pieces])


def body(node_feats, weight_one, weight_two, adj_tiles, tile_owner, tile_local, cotangent):
    nb, per, blk, _ = adj_tiles.shape
    nodes, width = node_feats.shape
    full = weight_one.shape[0]
    node_count = NX * NZ * NC
    index = lax.axis_index("nodes")
    y = lax.axis_index("feat")
    x, z, c = index // (NZ * NC), (index // NC) % NZ, index % NC
    bf, f32 = jnp.bfloat16, jnp.float32
    total = NX * NZ * nb

    tiles = adj_tiles.reshape(nb * per, blk, blk)
    column = (tile_owner * nb + tile_local)[:, 0]
    column_other = send(column, dc=1)
    tiles_other = send(tiles, dc=1)
    cot_other = send(cotangent, dc=1)

    def slots_of(columns):
        owner, local = columns // nb, columns % nb
        rx = (owner // (NZ * NC) - x) % NX
        rz = (owner // NC - z) % NZ
        mine = owner % NC == c
        ahead = (rz * NX + rx) * nb + local
        back = (rx * NZ + rz) * nb + local
        return jnp.where(mine, ahead, total), jnp.where(mine, back, total)

    ahead, back = slots_of(column)
    ahead_other, back_other = slots_of(column_other)

    def spread(features):
        pieces = gather_plane(features.reshape(nb, blk, width))
        mine, theirs = spread_call(ahead, ahead_other, tiles, tiles_other, pieces, total, nb)
        return mine + send(theirs, dc=1)

    terms = transposed_terms(back, back_other, tiles, tiles_other, cotangent, cot_other, total)
    turned = reduce_plane(terms, nb).astype(bf)

    order = (y + jnp.arange(NY)) % NY
    weight_in = weight_one.reshape(NY, width, full)[order].reshape(full, full)
    weight_back = weight_two.reshape(full, NY, width)[:, order].reshape(full, full)
    weight_out = lax.dynamic_slice_in_dim(weight_two, y * width, width, 1)

    prop_one = spread(node_feats).reshape(nodes, width).astype(bf)
    prop_full = jnp.concatenate(gather_y(prop_one), axis=1)
    z_one = jnp.dot(prop_full, weight_in, preferred_element_type=f32)
    sigma = jax.nn.sigmoid(z_one)
    hidden = (z_one * sigma).astype(bf)
    mixed = jnp.dot(hidden, weight_out, preferred_element_type=f32).astype(bf)
    layer_output = spread(mixed).reshape(nodes, width).astype(bf)

    turned_full = jnp.concatenate(gather_y(turned), axis=1)
    hidden_own = lax.dynamic_slice_in_dim(hidden, y * width, width, 1).reshape(nb, blk, width)
    factor = 1.0 / math.sqrt(nodes * node_count)
    grad_two = jnp.einsum("lih,lfi->hf", hidden_own, turned_full, preferred_element_type=f32)
    grad_hidden = jnp.einsum("lfi,hf->lih", turned_full, weight_back, preferred_element_type=f32).reshape(nodes, full)
    grad_z = (grad_hidden * sigma * (1.0 + z_one * (1.0 - sigma))).astype(bf)
    grad_one = lax.dot_general(prop_one, grad_z, (((0,), (0,)), ((), ())), preferred_element_type=f32)
    both = jnp.concatenate([grad_one, grad_two], axis=0) * factor
    summed = all_reduce(both.reshape(-1, width), index).reshape(2, width, full)
    inverse = (jnp.arange(NY) - y) % NY
    grad_two = summed[1].reshape(width, NY, width)[:, inverse].reshape(width, full)
    return (layer_output, summed[0], grad_two)


def solution(mesh):
    placed = (
        P("nodes", "feat"),
        P(),
        P(),
        P("nodes", None, None, None),
        P("nodes", None),
        P("nodes", None),
        P("nodes", "feat"),
    )
    return jax.shard_map(
        body,
        mesh=mesh,
        in_specs=placed,
        out_specs=(P("nodes", "feat"), P("feat", None), P("feat", None)),
        check_vma=False,
    )
```

```python
import functools
import math

import jax
import jax.numpy as jnp
from jax import lax
from jax.experimental import pallas as pl
from jax.experimental.pallas import tpu as pltpu
from jax.sharding import PartitionSpec as P


NX, NZ, NC, NY = 4, 8, 2, 4


STRIDE = 32
UNROLL = 6


def node_pairs(dx, dz, dc):
    pairs = []
    for x in range(NX):
        for z in range(NZ):
            for c in range(NC):
                there = (((x + dx) % NX) * NZ + (z + dz) % NZ) * NC + (c + dc) % NC
                pairs.append(((x * NZ + z) * NC + c, there))
    return pairs


def xor_pairs(bit):
    return [(i, i ^ bit) for i in range(NX * NZ * NC)]


def send(value, dx=0, dz=0, dc=0):
    return lax.ppermute(value, "nodes", node_pairs(dx, dz, dc))


def gather_y(value):
    pairs = [[(y, (y - r) % NY) for y in range(NY)] for r in range(NY)]
    return [value] + [lax.ppermute(value, "feat", pairs[r]) for r in range(1, NY)]


def ring_z(block):
    half = block.shape[0] // 2
    low, high = [block], [block]
    for _ in range(1, 4):
        low.append(send(low[-1], dz=1))
        high.append(send(high[-1], dz=-1))
    first = send(low[3][:half], dz=1)
    second = send(high[3][half:], dz=-1)
    return [[block], [high[1]], [high[2]], [high[3]], [first, second], [low[3]], [low[2]], [low[1]]]


def gather_plane(own):
    nb = own.shape[0]
    beside = [send(own, dx=-r) for r in (1, 2, 3)]
    pieces = []
    for shift, block in ((0, own), (nb, jnp.concatenate(beside, axis=0))):
        for r, parts in enumerate(ring_z(block)):
            at = r * NX * nb + shift
            for part in parts:
                pieces.append((at, part))
                at += part.shape[0]
    return pieces


def reduce_plane(parts, nb):
    f32, bf = jnp.float32, jnp.bfloat16
    half = NZ * nb // 2
    far = parts[2]
    up_far = send(far[:half], dx=1)
    down_far = send(far[half:], dx=-1)
    up = jnp.concatenate([(parts[1][:half].astype(f32) + up_far.astype(f32)).astype(bf), parts[1][half:]], axis=0)
    down = jnp.concatenate([parts[3][:half], (parts[3][half:].astype(f32) + down_far.astype(f32)).astype(bf)], axis=0)
    own = parts[0].astype(f32) + send(up, dx=1).astype(f32) + send(down, dx=-1).astype(f32)
    rows = [own[r * nb:(r + 1) * nb] for r in range(NZ)]
    cut = nb // 2
    up = send(rows[4][:cut].astype(bf), dz=1)
    down = send(rows[4][cut:].astype(bf), dz=-1)
    up = jnp.concatenate([(rows[3][:cut] + up.astype(f32)), rows[3][cut:]], axis=0).astype(bf)
    down = jnp.concatenate([rows[5][:cut], rows[5][cut:] + down.astype(f32)], axis=0).astype(bf)
    for r in (2, 1):
        up = (rows[r] + send(up, dz=1).astype(f32)).astype(bf)
        down = (rows[NZ - r] + send(down, dz=-1).astype(f32)).astype(bf)
    return rows[0] + send(up, dz=1).astype(f32) + send(down, dz=-1).astype(f32)


def all_reduce(value, index):
    cuts = []
    outer = (1, 16, 32)
    for bit in outer:
        half = value.shape[0] // 2
        upper = (index & bit) != 0
        mine = jnp.where(upper, value[half:], value[:half])
        give = jnp.where(upper, value[:half], value[half:])
        value = mine + lax.ppermute(give, "nodes", xor_pairs(bit))
        cuts.append(upper)
    for bit in (2, 4, 8):
        value = value + lax.ppermute(value, "nodes", xor_pairs(bit))
    for bit, upper in zip(reversed(outer), reversed(cuts)):
        other = lax.ppermute(value, "nodes", xor_pairs(bit))
        value = jnp.concatenate([jnp.where(upper, other, value), jnp.where(upper, value, other)], axis=0)
    return value


def plan_kernel(place, col_a, col_b, tile_list, ahead_list, back_list, counts, *, nb, per):
    bits = nb.bit_length() - 1
    x, z, c = place[0], place[1], place[2]
    total = NX * NZ * nb
    for s, cols in enumerate((col_a, col_b)):
        for b in range(nb):
            base = (s * nb + b) * STRIDE

            def one(k, n, cols=cols, b=b, base=base):
                column = cols[b * per + k]
                local = column & (nb - 1)
                owner = column >> bits
                rx = ((owner >> 4) - x) & (NX - 1)
                rz = ((owner >> 1) - z) & (NZ - 1)
                tile_list[base + n] = b * per + k
                ahead_list[base + n] = (rz * NX + rx) * nb + local
                back_list[base + n] = (rx * NZ + rz) * nb + local
                return n + jnp.where((owner & 1) == c, 1, 0)

            n = lax.fori_loop(0, per, one, 0)
            counts[s * nb + b] = n
            for j in range(UNROLL):
                tile_list[base + n + j] = 0
                ahead_list[base + n + j] = total
                back_list[base + n + j] = total


def plan_call(place, col_a, col_b, nb, per):
    shape = jax.ShapeDtypeStruct((2 * nb * STRIDE,), jnp.int32)
    smem = pl.BlockSpec(memory_space=pltpu.SMEM)
    return pl.pallas_call(
        functools.partial(plan_kernel, nb=nb, per=per),
        out_shape=[shape, shape, shape, jax.ShapeDtypeStruct((2 * nb,), jnp.int32)],
        in_specs=[smem] * 3,
        out_specs=[smem] * 4,
        name="plan",
    )(place, col_a, col_b)


def transposed_kernel(tile_list, back_list, counts, tiles_a, tiles_b, cot_a, cot_b, *rest):
    outs, (acc, held_a, held_b, sems) = rest[:NX], rest[NX:]
    blk = held_a.shape[1]
    rows = cot_a.shape[0] // blk
    copy_a = pltpu.make_async_copy(tiles_a, held_a, sems.at[0])
    copy_b = pltpu.make_async_copy(tiles_b, held_b, sems.at[1])
    copy_a.start()
    copy_b.start()
    acc[...] = jnp.zeros_like(acc)
    for s, (copy, tiles, cot) in enumerate(((copy_a, held_a, cot_a), (copy_b, held_b, cot_b))):
        copy.wait()
        for b in range(rows):
            turned = cot[b * blk:(b + 1) * blk, :].T
            base = (s * rows + b) * STRIDE

            def one(i, carry, tiles=tiles, turned=turned, base=base):
                for j in range(UNROLL // 2):
                    at = base + i * UNROLL + 2 * j
                    right = jnp.concatenate([tiles[tile_list[at]], tiles[tile_list[at + 1]]], axis=1)
                    term = jnp.dot(turned, right, preferred_element_type=jnp.float32)
                    one_slot, two_slot = back_list[at], back_list[at + 1]
                    acc[one_slot] = acc[one_slot] + term[:, :blk]
                    acc[two_slot] = acc[two_slot] + term[:, blk:]
                return carry

            lax.fori_loop(0, (counts[s * rows + b] + UNROLL - 1) // UNROLL, one, 0)
    size = outs[0].shape[0]
    for r, out in enumerate(outs):
        out[...] = acc[r * size:(r + 1) * size].astype(out.dtype)


def transposed_terms(lists, tiles_a, tiles_b, cot_a, cot_b, total):
    tile_list, _, back_list, counts = lists
    blk = tiles_a.shape[1]
    width = cot_a.shape[1]
    shape = jax.ShapeDtypeStruct((total // NX, width, blk), jnp.bfloat16)
    smem = pl.BlockSpec(memory_space=pltpu.SMEM)
    vmem = pl.BlockSpec(memory_space=pltpu.VMEM)
    free = pl.BlockSpec(memory_space=pl.ANY)
    return pl.pallas_call(
        transposed_kernel,
        out_shape=[shape] * NX,
        in_specs=[smem] * 3 + [free, free, vmem, vmem],
        out_specs=[vmem] * NX,
        scratch_shapes=[
            pltpu.VMEM((total + 1, width, blk), jnp.float32),
            pltpu.VMEM(tiles_a.shape, tiles_a.dtype),
            pltpu.VMEM(tiles_b.shape, tiles_b.dtype),
            pltpu.SemaphoreType.DMA((2,)),
        ],
        compiler_params=pltpu.CompilerParams(vmem_limit_bytes=32 * 1024 * 1024),
        name="transposed_terms",
    )(tile_list, back_list, counts, tiles_a, tiles_b, cot_a, cot_b)


def spread_call(lists, tiles_a, tiles_b, pieces, total, rows):
    tile_list, ahead_list, _, counts = lists
    blk = tiles_a.shape[1]
    width = pieces[0][1].shape[2]
    n = len(pieces)
    starts = [at for at, _ in pieces]
    sizes = [part.shape[0] for _, part in pieces]

    def kernel(tile_list, ahead_list, counts, tiles_a, tiles_b, *rest):
        parts, (out_a, out_b, held, held_a, held_b, sems) = rest[:n], rest[n:]
        copies = [
            pltpu.make_async_copy(part, held.at[pl.ds(at, size)], sems.at[i])
            for i, (part, at, size) in enumerate(zip(parts, starts, sizes))
        ]
        copy_a = pltpu.make_async_copy(tiles_a, held_a, sems.at[n])
        copy_b = pltpu.make_async_copy(tiles_b, held_b, sems.at[n + 1])
        for copy in copies:
            copy.start()
        copy_b.start()
        copy_a.start()
        held[total] = jnp.zeros_like(held[total])
        for copy in copies:
            copy.wait()
        for s, copy, tiles, out in ((1, copy_b, held_b, out_b), (0, copy_a, held_a, out_a)):
            copy.wait()
            for b in range(rows):
                base = (s * rows + b) * STRIDE

                def one(i, summed, tiles=tiles, base=base):
                    for j in range(UNROLL // 2):
                        at = base + i * UNROLL + 2 * j
                        left = jnp.concatenate([tiles[tile_list[at]], tiles[tile_list[at + 1]]], axis=1)
                        right = jnp.concatenate([held[ahead_list[at]], held[ahead_list[at + 1]]], axis=0)
                        summed = summed + jnp.dot(left, right, preferred_element_type=jnp.float32)
                    return summed

                zero = jnp.zeros((blk, width), jnp.float32)
                out[b] = lax.fori_loop(0, (counts[s * rows + b] + UNROLL - 1) // UNROLL, one, zero)

    shape = jax.ShapeDtypeStruct((rows, blk, width), jnp.float32)
    smem = pl.BlockSpec(memory_space=pltpu.SMEM)
    vmem = pl.BlockSpec(memory_space=pltpu.VMEM)
    free = pl.BlockSpec(memory_space=pl.ANY)
    return pl.pallas_call(
        kernel,
        out_shape=[shape, shape],
        in_specs=[smem] * 3 + [free] * (n + 2),
        out_specs=[vmem, vmem],
        scratch_shapes=[
            pltpu.VMEM((total + 1, blk, width), jnp.bfloat16),
            pltpu.VMEM(tiles_a.shape, tiles_a.dtype),
            pltpu.VMEM(tiles_b.shape, tiles_b.dtype),
            pltpu.SemaphoreType.DMA((n + 2,)),
        ],
        compiler_params=pltpu.CompilerParams(vmem_limit_bytes=24 * 1024 * 1024),
        name="spread",
    )(tile_list, ahead_list, counts, tiles_a, tiles_b, *[part for _, part in pieces])


def mixing_kernel(place, p0, p1, p2, p3, w_in, w_out, z_out, own_out, mixed_out):
    y = place[3]
    nodes, width = p0.shape
    blk = mixed_out.shape[1]
    for b in range(nodes // blk):
        at = slice(b * blk, (b + 1) * blk)
        z = None
        for r, part in enumerate((p0, p1, p2, p3)):
            row = pl.multiple_of(((y + r) & (NY - 1)) * width, width)
            term = jnp.dot(part[at, :], w_in[pl.ds(row, width), :], preferred_element_type=jnp.float32)
            z = term if z is None else z + term
        z_out[at, :] = z
        hidden = (z * jax.nn.sigmoid(z)).astype(jnp.bfloat16)
        mixed_out[b] = jnp.dot(hidden, w_out[...], preferred_element_type=jnp.float32).astype(jnp.bfloat16)
        own = z_out[at, pl.ds(pl.multiple_of(y * width, width), width)]
        own_out[at, :] = (own * jax.nn.sigmoid(own)).astype(jnp.bfloat16)


def mixing_call(place, parts, w_in, w_out, nb):
    nodes, width = parts[0].shape
    full = w_in.shape[0]
    smem = pl.BlockSpec(memory_space=pltpu.SMEM)
    vmem = pl.BlockSpec(memory_space=pltpu.VMEM)
    return pl.pallas_call(
        mixing_kernel,
        out_shape=[
            jax.ShapeDtypeStruct((nodes, full), jnp.float32),
            jax.ShapeDtypeStruct((nodes, width), jnp.bfloat16),
            jax.ShapeDtypeStruct((nb, nodes // nb, width), jnp.bfloat16),
        ],
        in_specs=[smem] + [vmem] * (NY + 2),
        out_specs=[vmem] * 3,
        compiler_params=pltpu.CompilerParams(vmem_limit_bytes=16 * 1024 * 1024),
        name="mixing",
    )(place, *parts, w_in, w_out)


def grads_kernel(place, z_all, prop, own, q0, q1, q2, q3, w_turned, out, *, factor):
    y = place[3]
    nodes, width = prop.shape
    blk = 128 if nodes % 128 == 0 else nodes
    down = (((0,), (0,)), ((), ()))
    first = None
    second = [None] * NY
    for b in range(nodes // blk):
        at = slice(b * blk, (b + 1) * blk)
        hidden_grad = None
        for r, part in enumerate((q0, q1, q2, q3)):
            row = pl.multiple_of(((y + r) & (NY - 1)) * width, width)
            term = jnp.dot(part[at, :], w_turned[pl.ds(row, width), :], preferred_element_type=jnp.float32)
            hidden_grad = term if hidden_grad is None else hidden_grad + term
            term = lax.dot_general(own[at, :], part[at, :], down, preferred_element_type=jnp.float32)
            second[r] = term if second[r] is None else second[r] + term
        z = z_all[at, :]
        sigma = jax.nn.sigmoid(z)
        grad_z = (hidden_grad * sigma * (1.0 + z * (1.0 - sigma))).astype(jnp.bfloat16)
        term = lax.dot_general(prop[at, :], grad_z, down, preferred_element_type=jnp.float32)
        first = term if first is None else first + term
    out[:width, :] = first * factor
    for r in range(NY):
        col = pl.multiple_of(((y + r) & (NY - 1)) * width, width)
        out[width:, pl.ds(col, width)] = second[r] * factor


def grads_call(place, z_all, prop, own, parts, w_turned, factor):
    width = prop.shape[1]
    full = w_turned.shape[0]
    smem = pl.BlockSpec(memory_space=pltpu.SMEM)
    vmem = pl.BlockSpec(memory_space=pltpu.VMEM)
    return pl.pallas_call(
        functools.partial(grads_kernel, factor=factor),
        out_shape=jax.ShapeDtypeStruct((2 * width, full), jnp.float32),
        in_specs=[smem] + [vmem] * (NY + 4),
        out_specs=vmem,
        compiler_params=pltpu.CompilerParams(vmem_limit_bytes=16 * 1024 * 1024),
        name="grads",
    )(place, z_all, prop, own, *parts, w_turned)


def step(node_feats, weight_one, weight_two, adj_tiles, tile_owner, tile_local, cotangent):
    nb, per, blk, _ = adj_tiles.shape
    nodes, width = node_feats.shape
    full = weight_one.shape[0]
    node_count = NX * NZ * NC
    index = lax.axis_index("nodes")
    y = lax.axis_index("feat")
    place = jnp.stack([index // (NZ * NC), (index // NC) % NZ, index % NC, y]).astype(jnp.int32)
    bf = jnp.bfloat16
    total = NX * NZ * nb

    tiles = adj_tiles.reshape(nb * per, blk, blk)
    column = (tile_owner * nb + tile_local)[:, 0]
    column_other = send(column, dc=1)
    tiles_other = send(tiles, dc=1)
    cot_other = send(cotangent, dc=1)
    lists = plan_call(place, column, column_other, nb, per)

    def spread(features):
        pieces = gather_plane(features)
        mine, theirs = spread_call(lists, tiles, tiles_other, pieces, total, nb)
        return (mine + send(theirs, dc=1)).reshape(nodes, width).astype(bf)

    terms = transposed_terms(lists, tiles, tiles_other, cotangent, cot_other, total)
    turned = jnp.swapaxes(reduce_plane(terms, nb), 1, 2).reshape(nodes, width).astype(bf)

    weight_out = lax.dynamic_slice_in_dim(weight_two, y * width, width, 1)
    prop_one = spread(node_feats.reshape(nb, blk, width))
    prop_parts = gather_y(prop_one)
    z_one, hidden_own, mixed = mixing_call(place, prop_parts, weight_one, weight_out, nb)
    layer_output = spread(mixed)

    turned_parts = gather_y(turned)
    factor = 1.0 / math.sqrt(nodes * node_count)
    both = grads_call(place, z_one, prop_one, hidden_own, turned_parts, weight_two.T, factor)
    summed = all_reduce(both.reshape(-1, width), index).reshape(2, width, full)
    return (layer_output, summed[0], summed[1])


def solution(mesh):
    placed = (
        P("nodes", "feat"),
        P(),
        P(),
        P("nodes", None, None, None),
        P("nodes", None),
        P("nodes", None),
        P("nodes", "feat"),
    )
    return jax.shard_map(
        step,
        mesh=mesh,
        in_specs=placed,
        out_specs=(P("nodes", "feat"), P("feat", None), P("feat", None)),
        check_vma=False,
    )
```

```python
import functools
import math

import jax
import jax.numpy as jnp
from jax import lax
from jax.experimental import pallas as pl
from jax.experimental.pallas import tpu as pltpu
from jax.sharding import PartitionSpec as P


NX, NZ, NC, NY = 4, 8, 2, 4


STRIDE = 32
UNROLL = 6


def node_pairs(dx, dz, dc):
    pairs = []
    for x in range(NX):
        for z in range(NZ):
            for c in range(NC):
                there = (((x + dx) % NX) * NZ + (z + dz) % NZ) * NC + (c + dc) % NC
                pairs.append(((x * NZ + z) * NC + c, there))
    return pairs


def xor_pairs(bit):
    return [(i, i ^ bit) for i in range(NX * NZ * NC)]


def send(value, dx=0, dz=0, dc=0):
    return lax.ppermute(value, "nodes", node_pairs(dx, dz, dc))


def gather_y(value):
    pairs = [[(y, (y - r) % NY) for y in range(NY)] for r in range(NY)]
    return [value] + [lax.ppermute(value, "feat", pairs[r]) for r in range(1, NY)]


def ring_z(block):
    half = block.shape[0] // 2
    low, high = [block], [block]
    for _ in range(1, 4):
        low.append(send(low[-1], dz=1))
        high.append(send(high[-1], dz=-1))
    first = send(low[3][:half], dz=1)
    second = send(high[3][half:], dz=-1)
    return [[block], [high[1]], [high[2]], [high[3]], [first, second], [low[3]], [low[2]], [low[1]]]


def gather_plane(own, extra=None):
    nb = own.shape[0]
    beside = [send(own, dx=-r) for r in (1, 2, 3)]
    block = own if extra is None else jnp.concatenate([own, extra], axis=0)
    pieces, extras = [], []
    for r, parts in enumerate(ring_z(block)):
        whole = 0
        for part in parts:
            count = min(part.shape[0], nb - whole)
            pieces.append((r * NX * nb + whole, count, part))
            if extra is not None and r and count < part.shape[0]:
                extras.append(part[count:])
            whole += count
    for r, parts in enumerate(ring_z(jnp.concatenate(beside, axis=0))):
        at = r * NX * nb + nb
        for part in parts:
            pieces.append((at, part.shape[0], part))
            at += part.shape[0]
    return pieces, extras


def reduce_plane(parts, nb):
    f32, bf = jnp.float32, jnp.bfloat16
    half = NZ * nb // 2
    far = parts[2]
    up_far = send(far[:half], dx=1)
    down_far = send(far[half:], dx=-1)
    up = jnp.concatenate([(parts[1][:half].astype(f32) + up_far.astype(f32)).astype(bf), parts[1][half:]], axis=0)
    down = jnp.concatenate([parts[3][:half], (parts[3][half:].astype(f32) + down_far.astype(f32)).astype(bf)], axis=0)
    own = parts[0].astype(f32) + send(up, dx=1).astype(f32) + send(down, dx=-1).astype(f32)
    rows = [own[r * nb:(r + 1) * nb] for r in range(NZ)]
    cut = nb // 2
    up = send(rows[4][:cut].astype(bf), dz=1)
    down = send(rows[4][cut:].astype(bf), dz=-1)
    up = jnp.concatenate([(rows[3][:cut] + up.astype(f32)), rows[3][cut:]], axis=0).astype(bf)
    down = jnp.concatenate([rows[5][:cut], rows[5][cut:] + down.astype(f32)], axis=0).astype(bf)
    for r in (2, 1):
        up = (rows[r] + send(up, dz=1).astype(f32)).astype(bf)
        down = (rows[NZ - r] + send(down, dz=-1).astype(f32)).astype(bf)
    return rows[0] + send(up, dz=1).astype(f32) + send(down, dz=-1).astype(f32)


def halve(value, index):
    value, give = value
    value = value + lax.ppermute(give, "nodes", xor_pairs(1))
    for bit in (16, 32):
        half = value.shape[0] // 2
        upper = (index & bit) != 0
        mine = jnp.where(upper, value[half:], value[:half])
        give = jnp.where(upper, value[:half], value[half:])
        value = mine + lax.ppermute(give, "nodes", xor_pairs(bit))
    return value


def double(value, index):
    for bit in (32, 16, 1):
        upper = (index & bit) != 0
        other = lax.ppermute(value, "nodes", xor_pairs(bit))
        value = jnp.concatenate([jnp.where(upper, other, value), jnp.where(upper, value, other)], axis=0)
    return value


def plan_kernel(place, col_a, col_b, lists, *, nb, per):
    bits = nb.bit_length() - 1
    x, z, c = place[0], place[1], place[2]
    total = NX * NZ * nb
    span = 2 * nb * STRIDE
    for s, cols in enumerate((col_a, col_b)):
        for b in range(nb):
            base = (s * nb + b) * STRIDE

            def one(k, n, cols=cols, b=b, base=base):
                column = cols[b * per + k]
                local = column & (nb - 1)
                owner = column >> bits
                rx = ((owner >> 4) - x) & (NX - 1)
                rz = ((owner >> 1) - z) & (NZ - 1)
                lists[base + n] = b * per + k
                lists[span + base + n] = (rz * NX + rx) * nb + local
                lists[2 * span + base + n] = (rx * NZ + rz) * nb + local
                return n + jnp.where((owner & 1) == c, 1, 0)

            n = lax.fori_loop(0, per, one, 0)
            lists[3 * span + s * nb + b] = (n + UNROLL - 1) // UNROLL
            for j in range(UNROLL):
                lists[base + n + j] = 0
                lists[span + base + n + j] = total
                lists[2 * span + base + n + j] = total


def plan_call(place, col_a, col_b, nb, per):
    smem = pl.BlockSpec(memory_space=pltpu.SMEM)
    return pl.pallas_call(
        functools.partial(plan_kernel, nb=nb, per=per),
        out_shape=jax.ShapeDtypeStruct((6 * nb * STRIDE + 128,), jnp.int32),
        in_specs=[smem] * 3,
        out_specs=smem,
        name="plan",
    )(place, col_a, col_b)


def transposed_kernel(lists, tiles_a, tiles_b, cot_a, cot_b, *rest):
    outs, (acc, held_a, held_b, sems) = rest[:NX], rest[NX:]
    blk = held_a.shape[1]
    rows = cot_a.shape[0] // blk
    span = 2 * rows * STRIDE
    copy_a = pltpu.make_async_copy(tiles_a, held_a, sems.at[0])
    copy_b = pltpu.make_async_copy(tiles_b, held_b, sems.at[1])
    copy_a.start()
    copy_b.start()
    acc[...] = jnp.zeros_like(acc)
    for s, (copy, tiles, cot) in enumerate(((copy_a, held_a, cot_a), (copy_b, held_b, cot_b))):
        copy.wait()
        for b in range(rows):
            turned = cot[b * blk:(b + 1) * blk, :].T
            base = (s * rows + b) * STRIDE

            def one(i, carry, tiles=tiles, turned=turned, base=base):
                for j in range(UNROLL // 2):
                    at = base + i * UNROLL + 2 * j
                    right = jnp.concatenate([tiles[lists[at]], tiles[lists[at + 1]]], axis=1)
                    term = jnp.dot(turned, right, preferred_element_type=jnp.float32)
                    one_slot, two_slot = lists[2 * span + at], lists[2 * span + at + 1]
                    acc[one_slot] = acc[one_slot] + term[:, :blk]
                    acc[two_slot] = acc[two_slot] + term[:, blk:]
                return carry

            lax.fori_loop(0, lists[3 * span + s * rows + b], one, 0)
    size = outs[0].shape[0]
    for r, out in enumerate(outs):
        out[...] = acc[r * size:(r + 1) * size].astype(out.dtype)


def transposed_terms(lists, tiles_a, tiles_b, cot_a, cot_b, total):
    blk = tiles_a.shape[1]
    width = cot_a.shape[1]
    shape = jax.ShapeDtypeStruct((total // NX, width, blk), jnp.bfloat16)
    smem = pl.BlockSpec(memory_space=pltpu.SMEM)
    vmem = pl.BlockSpec(memory_space=pltpu.VMEM)
    free = pl.BlockSpec(memory_space=pltpu.HBM)
    return pl.pallas_call(
        transposed_kernel,
        out_shape=[shape] * NX,
        in_specs=[smem, free, free, vmem, vmem],
        out_specs=[vmem] * NX,
        scratch_shapes=[
            pltpu.VMEM((total + 1, width, blk), jnp.float32),
            pltpu.VMEM(tiles_a.shape, tiles_a.dtype),
            pltpu.VMEM(tiles_b.shape, tiles_b.dtype),
            pltpu.SemaphoreType.DMA((2,)),
        ],
        compiler_params=pltpu.CompilerParams(vmem_limit_bytes=32 * 1024 * 1024),
        name="transposed_terms",
    )(lists, tiles_a, tiles_b, cot_a, cot_b)


def spread_call(lists, tiles_a, tiles_b, pieces, total, rows):
    blk = tiles_a.shape[1]
    width = pieces[0][2].shape[2]
    n = len(pieces)
    span = 2 * rows * STRIDE

    def kernel(lists, tiles_a, tiles_b, *rest):
        parts, (out_a, out_b, held, held_a, held_b, sems) = rest[:n], rest[n:]
        copies = [
            pltpu.make_async_copy(part.at[pl.ds(0, size)], held.at[pl.ds(at, size)], sems.at[i])
            for i, (part, (at, size, _)) in enumerate(zip(parts, pieces))
        ]
        copy_a = pltpu.make_async_copy(tiles_a, held_a, sems.at[n])
        copy_b = pltpu.make_async_copy(tiles_b, held_b, sems.at[n + 1])
        for copy in copies:
            copy.start()
        copy_b.start()
        copy_a.start()
        held[total] = jnp.zeros_like(held[total])
        for copy in copies:
            copy.wait()
        for s, copy, tiles, out in ((1, copy_b, held_b, out_b), (0, copy_a, held_a, out_a)):
            copy.wait()
            for b in range(rows):
                base = (s * rows + b) * STRIDE

                def one(i, summed, tiles=tiles, base=base):
                    for j in range(UNROLL // 2):
                        at = base + i * UNROLL + 2 * j
                        left = jnp.concatenate([tiles[lists[at]], tiles[lists[at + 1]]], axis=1)
                        one_slot, two_slot = lists[span + at], lists[span + at + 1]
                        right = jnp.concatenate([held[one_slot], held[two_slot]], axis=0)
                        summed = summed + jnp.dot(left, right, preferred_element_type=jnp.float32)
                    return summed

                zero = jnp.zeros((blk, width), jnp.float32)
                out[b] = lax.fori_loop(0, lists[3 * span + s * rows + b], one, zero)

    shape = jax.ShapeDtypeStruct((rows, blk, width), jnp.float32)
    smem = pl.BlockSpec(memory_space=pltpu.SMEM)
    vmem = pl.BlockSpec(memory_space=pltpu.VMEM)
    free = pl.BlockSpec(memory_space=pltpu.HBM)
    return pl.pallas_call(
        kernel,
        out_shape=[shape, shape],
        in_specs=[smem] + [free] * (n + 2),
        out_specs=[vmem, vmem],
        scratch_shapes=[
            pltpu.VMEM((total + 1, blk, width), jnp.bfloat16),
            pltpu.VMEM(tiles_a.shape, tiles_a.dtype),
            pltpu.VMEM(tiles_b.shape, tiles_b.dtype),
            pltpu.SemaphoreType.DMA((n + 2,)),
        ],
        compiler_params=pltpu.CompilerParams(vmem_limit_bytes=24 * 1024 * 1024),
        name="spread",
    )(lists, tiles_a, tiles_b, *[part for _, _, part in pieces])


def mixing_kernel(place, p0, p1, p2, p3, w_in, w_out, z_out, own_out, mixed_out):
    y = place[3]
    nodes, width = p0.shape
    blk = mixed_out.shape[1]
    for b in range(nodes // blk):
        at = slice(b * blk, (b + 1) * blk)
        z = None
        for r, part in enumerate((p0, p1, p2, p3)):
            row = pl.multiple_of(((y + r) & (NY - 1)) * width, width)
            term = jnp.dot(part[at, :], w_in[pl.ds(row, width), :], preferred_element_type=jnp.float32)
            z = term if z is None else z + term
        z_out[at, :] = z
        hidden = (z * jax.nn.sigmoid(z)).astype(jnp.bfloat16)
        mixed_out[b] = jnp.dot(hidden, w_out[...], preferred_element_type=jnp.float32).astype(jnp.bfloat16)
        own = z_out[at, pl.ds(pl.multiple_of(y * width, width), width)]
        own_out[at, :] = (own * jax.nn.sigmoid(own)).astype(jnp.bfloat16)


def mixing_call(place, parts, w_in, w_out, nb):
    nodes, width = parts[0].shape
    full = w_in.shape[0]
    smem = pl.BlockSpec(memory_space=pltpu.SMEM)
    vmem = pl.BlockSpec(memory_space=pltpu.VMEM)
    return pl.pallas_call(
        mixing_kernel,
        out_shape=[
            jax.ShapeDtypeStruct((nodes, full), jnp.float32),
            jax.ShapeDtypeStruct((nodes, width), jnp.bfloat16),
            jax.ShapeDtypeStruct((nb, nodes // nb, width), jnp.bfloat16),
        ],
        in_specs=[smem] + [vmem] * (NY + 2),
        out_specs=[vmem] * 3,
        compiler_params=pltpu.CompilerParams(vmem_limit_bytes=16 * 1024 * 1024),
        name="mixing",
    )(place, *parts, w_in, w_out)


def grads_kernel(place, z_all, prop, own, q0, q1, q2, q3, w_turned, keep, give, both, *, factor):
    y = place[3]
    nodes, width = prop.shape
    blk = 128 if nodes % 128 == 0 else nodes
    down = (((0,), (0,)), ((), ()))
    first = None
    second = [None] * NY
    for b in range(nodes // blk):
        at = slice(b * blk, (b + 1) * blk)
        hidden_grad = None
        for r, part in enumerate((q0, q1, q2, q3)):
            row = pl.multiple_of(((y + r) & (NY - 1)) * width, width)
            term = jnp.dot(part[at, :], w_turned[pl.ds(row, width), :], preferred_element_type=jnp.float32)
            hidden_grad = term if hidden_grad is None else hidden_grad + term
            term = lax.dot_general(own[at, :], part[at, :], down, preferred_element_type=jnp.float32)
            second[r] = term if second[r] is None else second[r] + term
        z = z_all[at, :]
        sigma = jax.nn.sigmoid(z)
        grad_z = (hidden_grad * sigma * (1.0 + z * (1.0 - sigma))).astype(jnp.bfloat16)
        term = lax.dot_general(prop[at, :], grad_z, down, preferred_element_type=jnp.float32)
        first = term if first is None else first + term
    both[0] = first * factor
    for r in range(NY):
        col = pl.multiple_of(((y + r) & (NY - 1)) * width, width)
        both[1, :, pl.ds(col, width)] = second[r] * factor
    mine = place[2]
    for r in range(NY):
        cols = slice(r * width, (r + 1) * width)
        rows = slice(r * width, (r + 1) * width)
        keep[rows, :] = both[mine, :, cols]
        give[rows, :] = both[1 - mine, :, cols]


def grads_call(place, z_all, prop, own, parts, w_turned, factor):
    width = prop.shape[1]
    full = w_turned.shape[0]
    smem = pl.BlockSpec(memory_space=pltpu.SMEM)
    vmem = pl.BlockSpec(memory_space=pltpu.VMEM)
    return pl.pallas_call(
        functools.partial(grads_kernel, factor=factor),
        out_shape=[jax.ShapeDtypeStruct((full, width), jnp.float32)] * 2,
        in_specs=[smem] + [vmem] * (NY + 4),
        out_specs=[vmem] * 2,
        scratch_shapes=[pltpu.VMEM((2, width, full), jnp.float32)],
        compiler_params=pltpu.CompilerParams(vmem_limit_bytes=16 * 1024 * 1024),
        name="grads",
    )(place, z_all, prop, own, *parts, w_turned)


def step(node_feats, weight_one, weight_two, adj_tiles, tile_owner, tile_local, cotangent):
    nb, per, blk, _ = adj_tiles.shape
    nodes, width = node_feats.shape
    full = weight_one.shape[0]
    node_count = NX * NZ * NC
    index = lax.axis_index("nodes")
    y = lax.axis_index("feat")
    place = jnp.stack([index // (NZ * NC), (index // NC) % NZ, index % NC, y]).astype(jnp.int32)
    bf = jnp.bfloat16
    total = NX * NZ * nb

    tiles = adj_tiles.reshape(nb * per, blk, blk)
    column = (tile_owner * nb + tile_local)[:, 0]
    column_other = send(column, dc=1)
    tiles_other = send(tiles, dc=1)
    cot_other = send(cotangent, dc=1)
    lists = plan_call(place, column, column_other, nb, per)

    def spread(features, extra=None):
        pieces, extras = gather_plane(features, extra)
        mine, theirs = spread_call(lists, tiles, tiles_other, pieces, total, nb)
        return (mine + send(theirs, dc=1)).reshape(nodes, width).astype(bf), extras

    terms = transposed_terms(lists, tiles, tiles_other, cotangent, cot_other, total)
    turned = jnp.swapaxes(reduce_plane(terms, nb), 1, 2).reshape(nodes, width).astype(bf)

    weight_out = lax.dynamic_slice_in_dim(weight_two, y * width, width, 1)
    prop_one, _ = spread(node_feats.reshape(nb, blk, width))
    prop_parts = gather_y(prop_one)
    z_one, hidden_own, mixed = mixing_call(place, prop_parts, weight_one, weight_out, nb)

    turned_parts = gather_y(turned)
    factor = 1.0 / math.sqrt(nodes * node_count)
    both = grads_call(place, z_one, prop_one, hidden_own, turned_parts, weight_two.T, factor)
    part = halve(both, index)
    high = part.astype(bf)
    low = (part - high.astype(jnp.float32)).astype(bf)
    layer_output, extras = spread(mixed, jnp.stack([high, low]))
    for extra in extras:
        part = part + extra[0].astype(jnp.float32) + extra[1].astype(jnp.float32)
    summed = double(part, index).reshape(2, NY, width, width)
    summed = jnp.swapaxes(summed, 1, 2).reshape(2, width, full)
    return (layer_output, summed[0], summed[1])


def solution(mesh):
    placed = (
        P("nodes", "feat"),
        P(),
        P(),
        P("nodes", None, None, None),
        P("nodes", None),
        P("nodes", None),
        P("nodes", "feat"),
    )
    return jax.shard_map(
        step,
        mesh=mesh,
        in_specs=placed,
        out_specs=(P("nodes", "feat"), P("feat", None), P("feat", None)),
        check_vma=False,
    )
```

```python
import functools
import math

import jax
import jax.numpy as jnp
from jax import lax
from jax.experimental import pallas as pl
from jax.experimental.pallas import tpu as pltpu
from jax.sharding import PartitionSpec as P


NX, NZ, NC, NY = 4, 8, 2, 4


STRIDE = 32
UNROLL = 6


def node_pairs(dx, dz, dc):
    pairs = []
    for x in range(NX):
        for z in range(NZ):
            for c in range(NC):
                there = (((x + dx) % NX) * NZ + (z + dz) % NZ) * NC + (c + dc) % NC
                pairs.append(((x * NZ + z) * NC + c, there))
    return pairs


def xor_pairs(bit):
    return [(i, i ^ bit) for i in range(NX * NZ * NC)]


def in_hbm(value):
    return pltpu.with_memory_space_constraint(value, pltpu.HBM)


def send(value, dx=0, dz=0, dc=0):
    return lax.ppermute(value, "nodes", node_pairs(dx, dz, dc))


def gather_y(value):
    pairs = [[(y, (y - r) % NY) for y in range(NY)] for r in range(NY)]
    return [value] + [lax.ppermute(value, "feat", pairs[r]) for r in range(1, NY)]


def ring_z(block):
    half = block.shape[0] // 2
    low, high = [block], [block]
    for _ in range(1, 4):
        low.append(send(low[-1], dz=1))
        high.append(send(high[-1], dz=-1))
    first = send(low[3][:half], dz=1)
    second = send(high[3][half:], dz=-1)
    return [[block], [high[1]], [high[2]], [high[3]], [first, second], [low[3]], [low[2]], [low[1]]]


def gather_plane(own, extra=None):
    nb = own.shape[0]
    beside = [send(own, dx=-r) for r in (1, 2, 3)]
    block = own if extra is None else jnp.concatenate([own, extra], axis=0)
    pieces, extras = [], []
    for r, parts in enumerate(ring_z(block)):
        whole = 0
        for part in parts:
            count = min(part.shape[0], nb - whole)
            pieces.append((r * NX * nb + whole, count, part))
            if extra is not None and r and count < part.shape[0]:
                extras.append(part[count:])
            whole += count
    for r, parts in enumerate(ring_z(jnp.concatenate(beside, axis=0))):
        at = r * NX * nb + nb
        for part in parts:
            pieces.append((at, part.shape[0], part))
            at += part.shape[0]
    return pieces, extras


def reduce_plane(parts, nb):
    f32, bf = jnp.float32, jnp.bfloat16
    half = NZ * nb // 2
    far = parts[2]
    up_far = send(far[:half], dx=1)
    down_far = send(far[half:], dx=-1)
    up_sum = (parts[1][:half].astype(f32) + up_far.astype(f32)).astype(bf)
    down_sum = (parts[3][half:].astype(f32) + down_far.astype(f32)).astype(bf)
    up = lax.dynamic_update_slice(parts[1], up_sum, (0, 0, 0))
    down = lax.dynamic_update_slice(parts[3], down_sum, (half, 0, 0))
    own = parts[0].astype(f32) + send(up, dx=1).astype(f32) + send(down, dx=-1).astype(f32)
    rows = [own[r * nb:(r + 1) * nb] for r in range(NZ)]
    cut = nb // 2
    up = send(rows[4][:cut].astype(bf), dz=1)
    down = send(rows[4][cut:].astype(bf), dz=-1)
    up = jnp.concatenate([(rows[3][:cut] + up.astype(f32)), rows[3][cut:]], axis=0).astype(bf)
    down = jnp.concatenate([rows[5][:cut], rows[5][cut:] + down.astype(f32)], axis=0).astype(bf)
    for r in (2, 1):
        up = (rows[r] + send(up, dz=1).astype(f32)).astype(bf)
        down = (rows[NZ - r] + send(down, dz=-1).astype(f32)).astype(bf)
    return rows[0] + send(up, dz=1).astype(f32) + send(down, dz=-1).astype(f32)


def halve(value, index):
    value, give = value
    value = value + lax.ppermute(give, "nodes", xor_pairs(1))
    for bit in (16, 32):
        half = value.shape[0] // 2
        upper = (index & bit) != 0
        mine = jnp.where(upper, value[half:], value[:half])
        give = jnp.where(upper, value[:half], value[half:])
        value = mine + lax.ppermute(give, "nodes", xor_pairs(bit))
    return value


def double(value, index):
    for bit in (32, 16, 1):
        upper = (index & bit) != 0
        other = lax.ppermute(value, "nodes", xor_pairs(bit))
        value = jnp.concatenate([jnp.where(upper, other, value), jnp.where(upper, value, other)], axis=0)
    return value


def plan_kernel(place, col_a, col_b, lists, *, nb, per):
    bits = nb.bit_length() - 1
    x, z, c = place[0], place[1], place[2]
    total = NX * NZ * nb
    span = 2 * nb * STRIDE
    for s, cols in enumerate((col_a, col_b)):
        for b in range(nb):
            base = (s * nb + b) * STRIDE

            def one(k, n, cols=cols, b=b, base=base):
                column = cols[b * per + k]
                local = column & (nb - 1)
                owner = column >> bits
                rx = ((owner >> 4) - x) & (NX - 1)
                rz = ((owner >> 1) - z) & (NZ - 1)
                lists[base + n] = b * per + k
                lists[span + base + n] = (rz * NX + rx) * nb + local
                lists[2 * span + base + n] = (rx * NZ + rz) * nb + local
                return n + jnp.where((owner & 1) == c, 1, 0)

            n = lax.fori_loop(0, per, one, 0)
            lists[3 * span + s * nb + b] = (n + UNROLL - 1) // UNROLL
            for j in range(UNROLL):
                lists[base + n + j] = 0
                lists[span + base + n + j] = total
                lists[2 * span + base + n + j] = total


def plan_call(place, col_a, col_b, nb, per):
    smem = pl.BlockSpec(memory_space=pltpu.SMEM)
    return pl.pallas_call(
        functools.partial(plan_kernel, nb=nb, per=per),
        out_shape=jax.ShapeDtypeStruct((6 * nb * STRIDE + 128,), jnp.int32),
        in_specs=[smem] * 3,
        out_specs=smem,
        name="plan",
    )(place, col_a, col_b)


def transposed_kernel(lists, tiles_a, tiles_b, cot_a, cot_b, *rest):
    outs, (acc, held_a, held_b, sems) = rest[:NX], rest[NX:]
    blk = held_a.shape[1]
    rows = cot_a.shape[0] // blk
    span = 2 * rows * STRIDE
    copy_a = pltpu.make_async_copy(tiles_a, held_a, sems.at[0])
    copy_b = pltpu.make_async_copy(tiles_b, held_b, sems.at[1])
    copy_a.start()
    copy_b.start()
    acc[...] = jnp.zeros_like(acc)
    for s, (copy, tiles, cot) in enumerate(((copy_a, held_a, cot_a), (copy_b, held_b, cot_b))):
        copy.wait()
        for b in range(rows):
            turned = cot[b * blk:(b + 1) * blk, :].T
            base = (s * rows + b) * STRIDE

            def one(i, carry, tiles=tiles, turned=turned, base=base):
                for j in range(UNROLL // 2):
                    at = base + i * UNROLL + 2 * j
                    right = jnp.concatenate([tiles[lists[at]], tiles[lists[at + 1]]], axis=1)
                    term = jnp.dot(turned, right, preferred_element_type=jnp.float32)
                    one_slot, two_slot = lists[2 * span + at], lists[2 * span + at + 1]
                    acc[one_slot] = acc[one_slot] + term[:, :blk]
                    acc[two_slot] = acc[two_slot] + term[:, blk:]
                return carry

            lax.fori_loop(0, lists[3 * span + s * rows + b], one, 0)
    size = outs[0].shape[0]
    for r, out in enumerate(outs):
        out[...] = acc[r * size:(r + 1) * size].astype(out.dtype)


def transposed_terms(lists, tiles_a, tiles_b, cot_a, cot_b, total):
    blk = tiles_a.shape[1]
    width = cot_a.shape[1]
    shape = jax.ShapeDtypeStruct((total // NX, width, blk), jnp.bfloat16)
    smem = pl.BlockSpec(memory_space=pltpu.SMEM)
    vmem = pl.BlockSpec(memory_space=pltpu.VMEM)
    free = pl.BlockSpec(memory_space=pltpu.HBM)
    return pl.pallas_call(
        transposed_kernel,
        out_shape=[shape] * NX,
        in_specs=[smem, free, free, vmem, vmem],
        out_specs=[vmem] * NX,
        scratch_shapes=[
            pltpu.VMEM((total + 1, width, blk), jnp.float32),
            pltpu.VMEM(tiles_a.shape, tiles_a.dtype),
            pltpu.VMEM(tiles_b.shape, tiles_b.dtype),
            pltpu.SemaphoreType.DMA((2,)),
        ],
        compiler_params=pltpu.CompilerParams(vmem_limit_bytes=32 * 1024 * 1024),
        name="transposed_terms",
    )(lists, in_hbm(tiles_a), in_hbm(tiles_b), cot_a, cot_b)


def spread_call(lists, tiles_a, tiles_b, pieces, total, rows):
    blk = tiles_a.shape[1]
    width = pieces[0][2].shape[2]
    n = len(pieces)
    span = 2 * rows * STRIDE

    def kernel(lists, tiles_a, tiles_b, *rest):
        parts, (out_a, out_b, held, held_a, held_b, sems) = rest[:n], rest[n:]
        copies = [
            pltpu.make_async_copy(part.at[pl.ds(0, size)], held.at[pl.ds(at, size)], sems.at[i])
            for i, (part, (at, size, _)) in enumerate(zip(parts, pieces))
        ]
        copy_a = pltpu.make_async_copy(tiles_a, held_a, sems.at[n])
        copy_b = pltpu.make_async_copy(tiles_b, held_b, sems.at[n + 1])
        for copy in copies:
            copy.start()
        copy_b.start()
        copy_a.start()
        held[total] = jnp.zeros_like(held[total])
        for copy in copies:
            copy.wait()
        for s, copy, tiles, out in ((1, copy_b, held_b, out_b), (0, copy_a, held_a, out_a)):
            copy.wait()
            for b in range(rows):
                base = (s * rows + b) * STRIDE

                def one(i, summed, tiles=tiles, base=base):
                    for j in range(UNROLL // 2):
                        at = base + i * UNROLL + 2 * j
                        left = jnp.concatenate([tiles[lists[at]], tiles[lists[at + 1]]], axis=1)
                        one_slot, two_slot = lists[span + at], lists[span + at + 1]
                        right = jnp.concatenate([held[one_slot], held[two_slot]], axis=0)
                        summed = summed + jnp.dot(left, right, preferred_element_type=jnp.float32)
                    return summed

                zero = jnp.zeros((blk, width), jnp.float32)
                out[b] = lax.fori_loop(0, lists[3 * span + s * rows + b], one, zero)

    shape = jax.ShapeDtypeStruct((rows, blk, width), jnp.float32)
    smem = pl.BlockSpec(memory_space=pltpu.SMEM)
    vmem = pl.BlockSpec(memory_space=pltpu.VMEM)
    free = pl.BlockSpec(memory_space=pltpu.HBM)
    return pl.pallas_call(
        kernel,
        out_shape=[shape, shape],
        in_specs=[smem] + [free] * (n + 2),
        out_specs=[vmem, vmem],
        scratch_shapes=[
            pltpu.VMEM((total + 1, blk, width), jnp.bfloat16),
            pltpu.VMEM(tiles_a.shape, tiles_a.dtype),
            pltpu.VMEM(tiles_b.shape, tiles_b.dtype),
            pltpu.SemaphoreType.DMA((n + 2,)),
        ],
        compiler_params=pltpu.CompilerParams(vmem_limit_bytes=24 * 1024 * 1024),
        name="spread",
    )(lists, in_hbm(tiles_a), in_hbm(tiles_b), *[in_hbm(part) for _, _, part in pieces])


def mixing_kernel(place, p0, p1, p2, p3, w_in, w_out, z_out, own_out, mixed_out):
    y = place[3]
    nodes, width = p0.shape
    blk = mixed_out.shape[1]
    for b in range(nodes // blk):
        at = slice(b * blk, (b + 1) * blk)
        z = None
        for r, part in enumerate((p0, p1, p2, p3)):
            row = pl.multiple_of(((y + r) & (NY - 1)) * width, width)
            term = jnp.dot(part[at, :], w_in[pl.ds(row, width), :], preferred_element_type=jnp.float32)
            z = term if z is None else z + term
        z_out[at, :] = z
        hidden = (z * jax.nn.sigmoid(z)).astype(jnp.bfloat16)
        mixed_out[b] = jnp.dot(hidden, w_out[...], preferred_element_type=jnp.float32).astype(jnp.bfloat16)
        own = z_out[at, pl.ds(pl.multiple_of(y * width, width), width)]
        own_out[at, :] = (own * jax.nn.sigmoid(own)).astype(jnp.bfloat16)


def mixing_call(place, parts, w_in, w_out, nb):
    nodes, width = parts[0].shape
    full = w_in.shape[0]
    smem = pl.BlockSpec(memory_space=pltpu.SMEM)
    vmem = pl.BlockSpec(memory_space=pltpu.VMEM)
    return pl.pallas_call(
        mixing_kernel,
        out_shape=[
            jax.ShapeDtypeStruct((nodes, full), jnp.float32),
            jax.ShapeDtypeStruct((nodes, width), jnp.bfloat16),
            jax.ShapeDtypeStruct((nb, nodes // nb, width), jnp.bfloat16),
        ],
        in_specs=[smem] + [vmem] * (NY + 2),
        out_specs=[vmem] * 3,
        compiler_params=pltpu.CompilerParams(vmem_limit_bytes=16 * 1024 * 1024),
        name="mixing",
    )(place, *parts, w_in, w_out)


def grads_kernel(place, z_all, prop, own, q0, q1, q2, q3, w_two, keep, give, both, *, factor):
    y = place[3]
    nodes, width = prop.shape
    blk = 128 if nodes % 128 == 0 else nodes
    down = (((0,), (0,)), ((), ()))
    across = (((1,), (1,)), ((), ()))
    first = None
    second = [None] * NY
    for b in range(nodes // blk):
        at = slice(b * blk, (b + 1) * blk)
        hidden_grad = None
        for r, part in enumerate((q0, q1, q2, q3)):
            col = pl.multiple_of(((y + r) & (NY - 1)) * width, width)
            term = lax.dot_general(part[at, :], w_two[:, pl.ds(col, width)], across, preferred_element_type=jnp.float32)
            hidden_grad = term if hidden_grad is None else hidden_grad + term
            term = lax.dot_general(own[at, :], part[at, :], down, preferred_element_type=jnp.float32)
            second[r] = term if second[r] is None else second[r] + term
        z = z_all[at, :]
        sigma = jax.nn.sigmoid(z)
        grad_z = (hidden_grad * sigma * (1.0 + z * (1.0 - sigma))).astype(jnp.bfloat16)
        term = lax.dot_general(prop[at, :], grad_z, down, preferred_element_type=jnp.float32)
        first = term if first is None else first + term
    both[0] = first * factor
    for r in range(NY):
        col = pl.multiple_of(((y + r) & (NY - 1)) * width, width)
        both[1, :, pl.ds(col, width)] = second[r] * factor
    mine = place[2]
    for r in range(NY):
        cols = slice(r * width, (r + 1) * width)
        rows = slice(r * width, (r + 1) * width)
        keep[rows, :] = both[mine, :, cols]
        give[rows, :] = both[1 - mine, :, cols]


def grads_call(place, z_all, prop, own, parts, w_two, factor):
    width = prop.shape[1]
    full = w_two.shape[0]
    smem = pl.BlockSpec(memory_space=pltpu.SMEM)
    vmem = pl.BlockSpec(memory_space=pltpu.VMEM)
    return pl.pallas_call(
        functools.partial(grads_kernel, factor=factor),
        out_shape=[jax.ShapeDtypeStruct((full, width), jnp.float32)] * 2,
        in_specs=[smem] + [vmem] * (NY + 4),
        out_specs=[vmem] * 2,
        scratch_shapes=[pltpu.VMEM((2, width, full), jnp.float32)],
        compiler_params=pltpu.CompilerParams(vmem_limit_bytes=16 * 1024 * 1024),
        name="grads",
    )(place, z_all, prop, own, *parts, w_two)


def step(node_feats, weight_one, weight_two, adj_tiles, tile_owner, tile_local, cotangent):
    nb, per, blk, _ = adj_tiles.shape
    nodes, width = node_feats.shape
    full = weight_one.shape[0]
    node_count = NX * NZ * NC
    index = lax.axis_index("nodes")
    y = lax.axis_index("feat")
    place = jnp.stack([index // (NZ * NC), (index // NC) % NZ, index % NC, y]).astype(jnp.int32)
    bf = jnp.bfloat16
    total = NX * NZ * nb

    tiles = adj_tiles.reshape(nb * per, blk, blk)
    column = (tile_owner * nb + tile_local)[:, 0]
    column_other = send(column, dc=1)
    tiles_other = send(tiles, dc=1)
    cot_other = send(cotangent, dc=1)
    lists = plan_call(place, column, column_other, nb, per)

    def spread(features, extra=None):
        pieces, extras = gather_plane(features, extra)
        mine, theirs = spread_call(lists, tiles, tiles_other, pieces, total, nb)
        return (mine + send(theirs, dc=1)).reshape(nodes, width).astype(bf), extras

    terms = transposed_terms(lists, tiles, tiles_other, cotangent, cot_other, total)
    turned = jnp.swapaxes(reduce_plane(terms, nb), 1, 2).reshape(nodes, width).astype(bf)

    weight_out = lax.dynamic_slice_in_dim(weight_two, y * width, width, 1)
    prop_one, _ = spread(node_feats.reshape(nb, blk, width))
    prop_parts = gather_y(prop_one)
    z_one, hidden_own, mixed = mixing_call(place, prop_parts, weight_one, weight_out, nb)

    turned_parts = gather_y(turned)
    factor = 1.0 / math.sqrt(nodes * node_count)
    both = grads_call(place, z_one, prop_one, hidden_own, turned_parts, weight_two, factor)
    part = halve(both, index)
    high = part.astype(bf)
    low = (part - high.astype(jnp.float32)).astype(bf)
    layer_output, extras = spread(mixed, jnp.stack([high, low]))
    for extra in extras:
        part = part + extra[0].astype(jnp.float32) + extra[1].astype(jnp.float32)
    summed = double(part, index).reshape(2, NY, width, width)
    summed = jnp.swapaxes(summed, 1, 2).reshape(2, width, full)
    return (layer_output, summed[0], summed[1])


def solution(mesh):
    placed = (
        P("nodes", "feat"),
        P(),
        P(),
        P("nodes", None, None, None),
        P("nodes", None),
        P("nodes", None),
        P("nodes", "feat"),
    )
    return jax.shard_map(
        step,
        mesh=mesh,
        in_specs=placed,
        out_specs=(P("nodes", "feat"), P("feat", None), P("feat", None)),
        check_vma=False,
    )
```

```python
import functools
import math

import jax
import jax.numpy as jnp
from jax import lax
from jax.experimental import pallas as pl
from jax.experimental.pallas import tpu as pltpu
from jax.sharding import PartitionSpec as P


NX, NZ, NC, NY = 4, 8, 2, 4


STRIDE = 32
UNROLL = 6
LATE = 8


def node_pairs(dx, dz, dc):
    pairs = []
    for x in range(NX):
        for z in range(NZ):
            for c in range(NC):
                there = (((x + dx) % NX) * NZ + (z + dz) % NZ) * NC + (c + dc) % NC
                pairs.append(((x * NZ + z) * NC + c, there))
    return pairs


def xor_pairs(bit):
    return [(i, i ^ bit) for i in range(NX * NZ * NC)]


def in_hbm(value):
    return pltpu.with_memory_space_constraint(value, pltpu.HBM)


def send(value, dx=0, dz=0, dc=0):
    return lax.ppermute(value, "nodes", node_pairs(dx, dz, dc))


def gather_y(value):
    pairs = [[(y, (y - r) % NY) for y in range(NY)] for r in range(NY)]
    return [value] + [lax.ppermute(value, "feat", pairs[r]) for r in range(1, NY)]


def gather_plane(own):
    beside = [send(own, dx=-r) for r in (1, 2, 3)]
    block = join_call([own] + beside)
    half = block.shape[0] // 2
    low, high = [block], [block]
    for _ in range(1, 4):
        low.append(send(low[-1], dz=1))
        high.append(send(high[-1], dz=-1))
    first = send(low[3][:half], dz=1)
    second = send(high[3][half:], dz=-1)
    return [block, high[1], high[2], high[3], None, low[3], low[2], low[1]], (first, second)


def join_call(parts):
    size, blk, width = parts[0].shape
    n = len(parts)

    def kernel(*refs):
        out, sems = refs[n], refs[n + 1]
        copies = [pltpu.make_async_copy(refs[i], out.at[pl.ds(i * size, size)], sems.at[i]) for i in range(n)]
        for copy in copies:
            copy.start()
        for copy in copies:
            copy.wait()

    free = pl.BlockSpec(memory_space=pl.ANY)
    return pl.pallas_call(
        kernel,
        out_shape=jax.ShapeDtypeStruct((n * size, blk, width), parts[0].dtype),
        in_specs=[free] * n,
        out_specs=free,
        scratch_shapes=[pltpu.SemaphoreType.DMA((n,))],
        name="join",
    )(*parts)


def reduce_plane(parts, nb):
    f32, bf = jnp.float32, jnp.bfloat16
    half = NZ * nb // 2
    far = parts[2]
    up_far = send(far[:half], dx=1)
    down_far = send(far[half:], dx=-1)
    up_sum = (parts[1][:half].astype(f32) + up_far.astype(f32)).astype(bf)
    down_sum = (parts[3][half:].astype(f32) + down_far.astype(f32)).astype(bf)
    up = lax.dynamic_update_slice(parts[1], up_sum, (0, 0, 0))
    down = lax.dynamic_update_slice(parts[3], down_sum, (half, 0, 0))
    own = parts[0].astype(f32) + send(up, dx=1).astype(f32) + send(down, dx=-1).astype(f32)
    for bit in (1, 2, 4):
        half = own.shape[0] // 2
        give = own[half:].astype(bf)
        own = own[:half] + lax.ppermute(give, "nodes", xor_pairs(bit * NC)).astype(f32)
    return own


def halve(value, index):
    value, give = value
    value = value + lax.ppermute(give, "nodes", xor_pairs(1))
    for bit in (16, 32):
        half = value.shape[0] // 2
        upper = (index & bit) != 0
        mine = jnp.where(upper, value[half:], value[:half])
        give = jnp.where(upper, value[:half], value[half:])
        value = mine + lax.ppermute(give, "nodes", xor_pairs(bit))
    for bit in (2, 4, 8):
        value = value + lax.ppermute(value, "nodes", xor_pairs(bit))
    return value


def double(value, index):
    for bit in (32, 16, 1):
        upper = (index & bit) != 0
        other = lax.ppermute(value, "nodes", xor_pairs(bit))
        value = jnp.concatenate([jnp.where(upper, other, value), jnp.where(upper, value, other)], axis=0)
    return value


def plan_offsets(nb):
    span = 2 * nb * STRIDE
    counts = 4 * span
    late = counts + 4 * nb
    return span, counts, late, late + 8 * LATE * 3


def plan_kernel(place, col_a, col_b, lists, *, nb, per):
    bits = nb.bit_length() - 1
    x, z, c = place[0], place[1], place[2]
    total = NX * NZ * nb
    span, counts, late, _ = plan_offsets(nb)
    for j in range(4 * LATE):
        lists[late + j] = 0
        lists[late + 4 * LATE + j] = NX * nb
        lists[late + 8 * LATE + j] = 0
    for s, cols in enumerate((col_a, col_b)):
        behind = 0
        for b in range(nb):
            base = (s * nb + b) * STRIDE

            def one(k, carry, cols=cols, b=b, base=base, s=s):
                early, every, behind = carry
                column = cols[b * per + k]
                local = column & (nb - 1)
                owner = column >> bits
                rx = ((owner >> 4) - x) & (NX - 1)
                zo = (owner >> 1) & (NZ - 1)
                rz = (zo - z) & (NZ - 1)
                rel = zo ^ z
                rank = ((rel & 1) << 2) | (rel & 2) | (rel >> 2)
                mine = jnp.where((owner & 1) == c, 1, 0)
                far = jnp.where(rz == NZ // 2, mine, 0)
                lists[base + early] = b * per + k
                lists[span + base + early] = (rz * NX + rx) * nb + local
                lists[2 * span + base + every] = b * per + k
                lists[3 * span + base + every] = (rx * NZ + rank) * nb + local
                at = late + 2 * LATE * s + behind
                lists[at] = b * per + k
                lists[at + 4 * LATE] = rx * nb + local
                lists[at + 8 * LATE] = b
                return early + mine - far, every + mine, behind + far

            early, every, behind = lax.fori_loop(0, per, one, (0, 0, behind))
            lists[counts + s * nb + b] = (early + UNROLL - 1) // UNROLL
            lists[counts + 2 * nb + s * nb + b] = (every + UNROLL - 1) // UNROLL
            for j in range(UNROLL):
                lists[base + early + j] = 0
                lists[span + base + early + j] = total
                lists[2 * span + base + every + j] = 0
                lists[3 * span + base + every + j] = total
        at = late + 2 * LATE * s + behind
        lists[at] = 0
        lists[at + 4 * LATE] = NX * nb
        lists[at + 8 * LATE] = 0


def plan_call(place, col_a, col_b, nb, per):
    smem = pl.BlockSpec(memory_space=pltpu.SMEM)
    return pl.pallas_call(
        functools.partial(plan_kernel, nb=nb, per=per),
        out_shape=jax.ShapeDtypeStruct((plan_offsets(nb)[3],), jnp.int32),
        in_specs=[smem] * 3,
        out_specs=smem,
        name="plan",
    )(place, col_a, col_b)


def transposed_kernel(lists, tiles_a, tiles_b, cot_a, cot_b, *rest):
    outs, (acc, held_a, held_b, sems) = rest[:NX], rest[NX:]
    blk = held_a.shape[1]
    rows = cot_a.shape[0] // blk
    span, counts, _, _ = plan_offsets(rows)
    copy_a = pltpu.make_async_copy(tiles_a, held_a, sems.at[0])
    copy_b = pltpu.make_async_copy(tiles_b, held_b, sems.at[1])
    copy_a.start()
    copy_b.start()
    acc[...] = jnp.zeros_like(acc)
    for s, (copy, tiles, cot) in enumerate(((copy_a, held_a, cot_a), (copy_b, held_b, cot_b))):
        copy.wait()
        for b in range(rows):
            turned = cot[b * blk:(b + 1) * blk, :].T
            base = (s * rows + b) * STRIDE

            def one(i, carry, tiles=tiles, turned=turned, base=base):
                for j in range(UNROLL // 2):
                    at = base + i * UNROLL + 2 * j
                    one_tile, two_tile = lists[2 * span + at], lists[2 * span + at + 1]
                    right = jnp.concatenate([tiles[one_tile], tiles[two_tile]], axis=1)
                    term = jnp.dot(turned, right, preferred_element_type=jnp.float32)
                    one_slot, two_slot = lists[3 * span + at], lists[3 * span + at + 1]
                    acc[one_slot] = acc[one_slot] + term[:, :blk]
                    acc[two_slot] = acc[two_slot] + term[:, blk:]
                return carry

            lax.fori_loop(0, lists[counts + 2 * rows + s * rows + b], one, 0)
    size = outs[0].shape[0]
    for r, out in enumerate(outs):
        out[...] = acc[r * size:(r + 1) * size].astype(out.dtype)


def transposed_terms(lists, tiles_a, tiles_b, cot_a, cot_b, total):
    blk = tiles_a.shape[1]
    width = cot_a.shape[1]
    shape = jax.ShapeDtypeStruct((total // NX, width, blk), jnp.bfloat16)
    smem = pl.BlockSpec(memory_space=pltpu.SMEM)
    vmem = pl.BlockSpec(memory_space=pltpu.VMEM)
    free = pl.BlockSpec(memory_space=pltpu.HBM)
    return pl.pallas_call(
        transposed_kernel,
        out_shape=[shape] * NX,
        in_specs=[smem, free, free, vmem, vmem],
        out_specs=[vmem] * NX,
        scratch_shapes=[
            pltpu.VMEM((total + 1, width, blk), jnp.float32),
            pltpu.VMEM(tiles_a.shape, tiles_a.dtype),
            pltpu.VMEM(tiles_b.shape, tiles_b.dtype),
            pltpu.SemaphoreType.DMA((2,)),
        ],
        compiler_params=pltpu.CompilerParams(vmem_limit_bytes=32 * 1024 * 1024),
        name="transposed_terms",
    )(lists, in_hbm(tiles_a), in_hbm(tiles_b), cot_a, cot_b)


def early_call(lists, tiles_a, tiles_b, pieces, total, rows):
    blk = tiles_a.shape[1]
    size, _, width = pieces[0].shape
    offsets = [r for r, part in enumerate(pieces) if part is not None]
    n = len(offsets)
    span, counts, _, _ = plan_offsets(rows)

    def kernel(lists, tiles_a, tiles_b, *rest):
        parts, (out_a, out_b, held, held_a, held_b, sems) = rest[:n], rest[n:]
        copies = [
            pltpu.make_async_copy(part, held.at[pl.ds(r * size, size)], sems.at[i])
            for i, (part, r) in enumerate(zip(parts, offsets))
        ]
        copy_a = pltpu.make_async_copy(tiles_a, held_a, sems.at[n])
        copy_b = pltpu.make_async_copy(tiles_b, held_b, sems.at[n + 1])
        for copy in copies:
            copy.start()
        copy_b.start()
        copy_a.start()
        held[total] = jnp.zeros_like(held[total])
        for copy in copies:
            copy.wait()
        for s, copy, tiles, out in ((1, copy_b, held_b, out_b), (0, copy_a, held_a, out_a)):
            copy.wait()
            for b in range(rows):
                base = (s * rows + b) * STRIDE

                def one(i, summed, tiles=tiles, base=base):
                    for j in range(UNROLL // 2):
                        at = base + i * UNROLL + 2 * j
                        left = jnp.concatenate([tiles[lists[at]], tiles[lists[at + 1]]], axis=1)
                        one_slot, two_slot = lists[span + at], lists[span + at + 1]
                        right = jnp.concatenate([held[one_slot], held[two_slot]], axis=0)
                        summed = summed + jnp.dot(left, right, preferred_element_type=jnp.float32)
                    return summed

                zero = jnp.zeros((blk, width), jnp.float32)
                out[b] = lax.fori_loop(0, lists[counts + s * rows + b], one, zero)

    shape = jax.ShapeDtypeStruct((rows, blk, width), jnp.float32)
    smem = pl.BlockSpec(memory_space=pltpu.SMEM)
    vmem = pl.BlockSpec(memory_space=pltpu.VMEM)
    free = pl.BlockSpec(memory_space=pltpu.HBM)
    return pl.pallas_call(
        kernel,
        out_shape=[shape, shape],
        in_specs=[smem] + [free] * (n + 2),
        out_specs=[vmem, vmem],
        scratch_shapes=[
            pltpu.VMEM((total + 1, blk, width), jnp.bfloat16),
            pltpu.VMEM(tiles_a.shape, tiles_a.dtype),
            pltpu.VMEM(tiles_b.shape, tiles_b.dtype),
            pltpu.SemaphoreType.DMA((n + 2,)),
        ],
        compiler_params=pltpu.CompilerParams(vmem_limit_bytes=24 * 1024 * 1024),
        name="early",
    )(lists, in_hbm(tiles_a), in_hbm(tiles_b), *[in_hbm(pieces[r]) for r in offsets])


def late_kernel(lists, tiles_a, tiles_b, first, second, early_a, early_b, out_a, out_b, held, got, sems):
    rows = early_a.shape[0]
    half = first.shape[0]
    _, _, late, _ = plan_offsets(rows)
    copies = [
        pltpu.make_async_copy(first, held.at[pl.ds(0, half)], sems.at[0]),
        pltpu.make_async_copy(second, held.at[pl.ds(half, half)], sems.at[1]),
    ]
    for s, tiles in ((0, tiles_a), (1, tiles_b)):
        for j in range(LATE):
            at = s * LATE + j
            copies.append(pltpu.make_async_copy(tiles.at[lists[late + 2 * LATE * s + j]], got.at[at], sems.at[2 + at]))
    for copy in copies:
        copy.start()
    held[2 * half] = jnp.zeros_like(held[2 * half])
    out_a[...] = early_a[...]
    out_b[...] = early_b[...]
    for copy in copies:
        copy.wait()
    for s, out in ((0, out_a), (1, out_b)):
        for j in range(LATE):
            at = late + 2 * LATE * s + j
            term = jnp.dot(got[s * LATE + j], held[lists[at + 4 * LATE]], preferred_element_type=jnp.float32)
            row = lists[at + 8 * LATE]
            out[row] = out[row] + term


def late_call(lists, tiles_a, tiles_b, last, early):
    rows, blk, width = early[0].shape
    shape = jax.ShapeDtypeStruct((rows, blk, width), jnp.float32)
    smem = pl.BlockSpec(memory_space=pltpu.SMEM)
    vmem = pl.BlockSpec(memory_space=pltpu.VMEM)
    free = pl.BlockSpec(memory_space=pl.ANY)
    tiled = pl.BlockSpec(memory_space=pltpu.HBM)
    return pl.pallas_call(
        late_kernel,
        out_shape=[shape, shape],
        in_specs=[smem, tiled, tiled, free, free, vmem, vmem],
        out_specs=[vmem, vmem],
        scratch_shapes=[
            pltpu.VMEM((2 * last[0].shape[0] + 1, blk, width), jnp.bfloat16),
            pltpu.VMEM((2 * LATE, blk, blk), tiles_a.dtype),
            pltpu.SemaphoreType.DMA((2 + 2 * LATE,)),
        ],
        compiler_params=pltpu.CompilerParams(vmem_limit_bytes=8 * 1024 * 1024),
        name="late",
    )(lists, in_hbm(tiles_a), in_hbm(tiles_b), *last, *early)


def mixing_kernel(place, p0, p1, p2, p3, w_in, w_out, z_out, own_out, mixed_out):
    y = place[3]
    nodes, width = p0.shape
    blk = mixed_out.shape[1]
    for b in range(nodes // blk):
        at = slice(b * blk, (b + 1) * blk)
        z = None
        for r, part in enumerate((p0, p1, p2, p3)):
            row = pl.multiple_of(((y + r) & (NY - 1)) * width, width)
            term = jnp.dot(part[at, :], w_in[pl.ds(row, width), :], preferred_element_type=jnp.float32)
            z = term if z is None else z + term
        z_out[at, :] = z
        hidden = (z * jax.nn.sigmoid(z)).astype(jnp.bfloat16)
        mixed_out[b] = jnp.dot(hidden, w_out[...], preferred_element_type=jnp.float32).astype(jnp.bfloat16)
        own = z_out[at, pl.ds(pl.multiple_of(y * width, width), width)]
        own_out[at, :] = (own * jax.nn.sigmoid(own)).astype(jnp.bfloat16)


def mixing_call(place, parts, w_in, w_out, nb):
    nodes, width = parts[0].shape
    full = w_in.shape[0]
    smem = pl.BlockSpec(memory_space=pltpu.SMEM)
    vmem = pl.BlockSpec(memory_space=pltpu.VMEM)
    return pl.pallas_call(
        mixing_kernel,
        out_shape=[
            jax.ShapeDtypeStruct((nodes, full), jnp.float32),
            jax.ShapeDtypeStruct((nodes, width), jnp.bfloat16),
            jax.ShapeDtypeStruct((nb, nodes // nb, width), jnp.bfloat16),
        ],
        in_specs=[smem] + [vmem] * (NY + 2),
        out_specs=[vmem] * 3,
        compiler_params=pltpu.CompilerParams(vmem_limit_bytes=16 * 1024 * 1024),
        name="mixing",
    )(place, *parts, w_in, w_out)


def grads_kernel(place, z_all, prop, own, q0, q1, q2, q3, w_two, keep, give, both, *, factor):
    y = place[3]
    nodes, width = prop.shape
    blk = 128 if nodes % 128 == 0 else nodes
    down = (((0,), (0,)), ((), ()))
    across = (((1,), (1,)), ((), ()))
    first = None
    second = [None] * NY
    for b in range(nodes // blk):
        at = slice(b * blk, (b + 1) * blk)
        hidden_grad = None
        for r, part in enumerate((q0, q1, q2, q3)):
            col = pl.multiple_of(((y + r) & (NY - 1)) * width, width)
            term = lax.dot_general(part[at, :], w_two[:, pl.ds(col, width)], across, preferred_element_type=jnp.float32)
            hidden_grad = term if hidden_grad is None else hidden_grad + term
            term = lax.dot_general(own[at, :], part[at, :], down, preferred_element_type=jnp.float32)
            second[r] = term if second[r] is None else second[r] + term
        z = z_all[at, :]
        sigma = jax.nn.sigmoid(z)
        grad_z = (hidden_grad * sigma * (1.0 + z * (1.0 - sigma))).astype(jnp.bfloat16)
        term = lax.dot_general(prop[at, :], grad_z, down, preferred_element_type=jnp.float32)
        first = term if first is None else first + term
    both[0] = first * factor
    for r in range(NY):
        col = pl.multiple_of(((y + r) & (NY - 1)) * width, width)
        both[1, :, pl.ds(col, width)] = second[r] * factor
    mine = place[2]
    for r in range(NY):
        cols = slice(r * width, (r + 1) * width)
        rows = slice(r * width, (r + 1) * width)
        keep[rows, :] = both[mine, :, cols]
        give[rows, :] = both[1 - mine, :, cols]


def grads_call(place, z_all, prop, own, parts, w_two, factor):
    width = prop.shape[1]
    full = w_two.shape[0]
    smem = pl.BlockSpec(memory_space=pltpu.SMEM)
    vmem = pl.BlockSpec(memory_space=pltpu.VMEM)
    return pl.pallas_call(
        functools.partial(grads_kernel, factor=factor),
        out_shape=[jax.ShapeDtypeStruct((full, width), jnp.float32)] * 2,
        in_specs=[smem] + [vmem] * (NY + 4),
        out_specs=[vmem] * 2,
        scratch_shapes=[pltpu.VMEM((2, width, full), jnp.float32)],
        compiler_params=pltpu.CompilerParams(vmem_limit_bytes=16 * 1024 * 1024),
        name="grads",
    )(place, z_all, prop, own, *parts, w_two)


def step(node_feats, weight_one, weight_two, adj_tiles, tile_owner, tile_local, cotangent):
    nb, per, blk, _ = adj_tiles.shape
    nodes, width = node_feats.shape
    full = weight_one.shape[0]
    node_count = NX * NZ * NC
    index = lax.axis_index("nodes")
    y = lax.axis_index("feat")
    place = jnp.stack([index // (NZ * NC), (index // NC) % NZ, index % NC, y]).astype(jnp.int32)
    bf = jnp.bfloat16
    total = NX * NZ * nb

    tiles = adj_tiles.reshape(nb * per, blk, blk)
    column = (tile_owner * nb + tile_local)[:, 0]
    column_other = send(column, dc=1)
    tiles_other = send(tiles, dc=1)
    cot_other = send(cotangent, dc=1)
    lists = plan_call(place, column, column_other, nb, per)

    def spread(features):
        pieces, last = gather_plane(features)
        early = early_call(lists, tiles, tiles_other, pieces, total, nb)
        mine, theirs = late_call(lists, tiles, tiles_other, last, early)
        return (mine + send(theirs, dc=1)).reshape(nodes, width).astype(bf)

    terms = transposed_terms(lists, tiles, tiles_other, cotangent, cot_other, total)
    turned = jnp.swapaxes(reduce_plane(terms, nb), 1, 2).reshape(nodes, width).astype(bf)

    weight_out = lax.dynamic_slice_in_dim(weight_two, y * width, width, 1)
    prop_one = spread(node_feats.reshape(nb, blk, width))
    prop_parts = gather_y(prop_one)
    z_one, hidden_own, mixed = mixing_call(place, prop_parts, weight_one, weight_out, nb)

    turned_parts = gather_y(turned)
    factor = 1.0 / math.sqrt(nodes * node_count)
    both = grads_call(place, z_one, prop_one, hidden_own, turned_parts, weight_two, factor)
    part = halve(both, index)
    layer_output = spread(mixed)
    summed = double(part, index).reshape(2, NY, width, width)
    summed = jnp.swapaxes(summed, 1, 2).reshape(2, width, full)
    return (layer_output, summed[0], summed[1])


def solution(mesh):
    placed = (
        P("nodes", "feat"),
        P(),
        P(),
        P("nodes", None, None, None),
        P("nodes", None),
        P("nodes", None),
        P("nodes", "feat"),
    )
    return jax.shard_map(
        step,
        mesh=mesh,
        in_specs=placed,
        out_specs=(P("nodes", "feat"), P("feat", None), P("feat", None)),
        check_vma=False,
    )
```

```python
import functools
import math

import jax
import jax.numpy as jnp
from jax import lax
from jax.experimental import pallas as pl
from jax.experimental.pallas import tpu as pltpu
from jax.sharding import PartitionSpec as P


NX, NZ, NC, NY = 4, 8, 2, 4


STRIDE = 32
UNROLL = 6
LATE = 8


def node_pairs(dx, dz, dc):
    pairs = []
    for x in range(NX):
        for z in range(NZ):
            for c in range(NC):
                there = (((x + dx) % NX) * NZ + (z + dz) % NZ) * NC + (c + dc) % NC
                pairs.append(((x * NZ + z) * NC + c, there))
    return pairs


def xor_pairs(bit):
    return [(i, i ^ bit) for i in range(NX * NZ * NC)]


def in_hbm(value):
    return pltpu.with_memory_space_constraint(value, pltpu.HBM)


def send(value, dx=0, dz=0, dc=0):
    return lax.ppermute(value, "nodes", node_pairs(dx, dz, dc))


def gather_y(value):
    pairs = [[(y, (y - r) % NY) for y in range(NY)] for r in range(NY)]
    return [value] + [lax.ppermute(value, "feat", pairs[r]) for r in range(1, NY)]


def ring_z(block):
    half = block.shape[0] // 2
    low, high = [block], [block]
    for _ in range(1, 4):
        low.append(send(low[-1], dz=1))
        high.append(send(high[-1], dz=-1))
    first = send(low[3][:half], dz=1)
    second = send(high[3][half:], dz=-1)
    return [block, high[1], high[2], high[3], (first, second), low[3], low[2], low[1]]


def gather_plane(own, extra=None):
    nb = own.shape[0]
    beside = [send(own, dx=-r) for r in (1, 2, 3)]
    if extra is None:
        rings = [(0, NX * nb, ring_z(join_call([own] + beside)))]
    else:
        others = ring_z(join_call(beside))
        rings = [(0, nb, ring_z(jnp.concatenate([own, extra], axis=0))), (nb, 3 * nb, others)]
    near, last, extras = [], [], []
    for shift, count, ring in rings:
        for r, entry in enumerate(ring):
            if r == NZ // 2:
                half = entry[0].shape[0]
                last.append((shift, half, entry[0]))
                last.append((shift + half, count - half, entry[1]))
                tail = entry[1][count - half:]
            else:
                near.append((r * NX * nb + shift, count, entry))
                tail = entry[count:]
            if extra is not None and shift == 0 and r:
                extras.append(tail)
    return near, last, extras


def join_call(parts):
    size, blk, width = parts[0].shape
    n = len(parts)

    def kernel(*refs):
        for i in range(n):
            refs[n][i * size:(i + 1) * size] = refs[i][...]

    vmem = pl.BlockSpec(memory_space=pltpu.VMEM)
    return pl.pallas_call(
        kernel,
        out_shape=jax.ShapeDtypeStruct((n * size, blk, width), parts[0].dtype),
        in_specs=[vmem] * n,
        out_specs=vmem,
        compiler_params=pltpu.CompilerParams(vmem_limit_bytes=4 * 1024 * 1024),
        name="join",
    )(*parts)


def reduce_plane(parts, nb):
    f32, bf = jnp.float32, jnp.bfloat16
    half = NZ * nb // 2
    far = parts[2]
    up_far = send(far[:half], dx=1)
    down_far = send(far[half:], dx=-1)
    up_sum = (parts[1][:half].astype(f32) + up_far.astype(f32)).astype(bf)
    down_sum = (parts[3][half:].astype(f32) + down_far.astype(f32)).astype(bf)
    up = lax.dynamic_update_slice(parts[1], up_sum, (0, 0, 0))
    down = lax.dynamic_update_slice(parts[3], down_sum, (half, 0, 0))
    own = parts[0].astype(f32) + send(up, dx=1).astype(f32) + send(down, dx=-1).astype(f32)
    for bit in (1, 2, 4):
        half = own.shape[0] // 2
        give = own[half:].astype(bf)
        own = own[:half] + lax.ppermute(give, "nodes", xor_pairs(bit * NC)).astype(f32)
    return own


def halve(value, index):
    value, give = value
    value = value + lax.ppermute(give, "nodes", xor_pairs(1))
    for bit in (16, 32):
        half = value.shape[0] // 2
        upper = (index & bit) != 0
        mine = jnp.where(upper, value[half:], value[:half])
        give = jnp.where(upper, value[:half], value[half:])
        value = mine + lax.ppermute(give, "nodes", xor_pairs(bit))
    return value


def double(value, index):
    for bit in (32, 16, 1):
        upper = (index & bit) != 0
        other = lax.ppermute(value, "nodes", xor_pairs(bit))
        value = jnp.concatenate([jnp.where(upper, other, value), jnp.where(upper, value, other)], axis=0)
    return value


def plan_offsets(nb):
    span = 2 * nb * STRIDE
    counts = 4 * span
    late = counts + 4 * nb
    return span, counts, late, late + 8 * LATE * 3


def plan_kernel(place, col_a, col_b, lists, *, nb, per):
    bits = nb.bit_length() - 1
    x, z, c = place[0], place[1], place[2]
    total = NX * NZ * nb
    span, counts, late, _ = plan_offsets(nb)
    for j in range(4 * LATE):
        lists[late + j] = 0
        lists[late + 4 * LATE + j] = NX * nb
        lists[late + 8 * LATE + j] = 0
    for s, cols in enumerate((col_a, col_b)):
        behind = 0
        for b in range(nb):
            base = (s * nb + b) * STRIDE

            def one(k, carry, cols=cols, b=b, base=base, s=s):
                early, every, behind = carry
                column = cols[b * per + k]
                local = column & (nb - 1)
                owner = column >> bits
                rx = ((owner >> 4) - x) & (NX - 1)
                zo = (owner >> 1) & (NZ - 1)
                rz = (zo - z) & (NZ - 1)
                rel = zo ^ z
                rank = ((rel & 1) << 2) | (rel & 2) | (rel >> 2)
                mine = jnp.where((owner & 1) == c, 1, 0)
                far = jnp.where(rz == NZ // 2, mine, 0)
                lists[base + early] = b * per + k
                lists[span + base + early] = (rz * NX + rx) * nb + local
                lists[2 * span + base + every] = b * per + k
                lists[3 * span + base + every] = (rx * NZ + rank) * nb + local
                at = late + 2 * LATE * s + behind
                lists[at] = b * per + k
                lists[at + 4 * LATE] = rx * nb + local
                lists[at + 8 * LATE] = b
                return early + mine - far, every + mine, behind + far

            early, every, behind = lax.fori_loop(0, per, one, (0, 0, behind))
            lists[counts + s * nb + b] = (early + UNROLL - 1) // UNROLL
            lists[counts + 2 * nb + s * nb + b] = (every + UNROLL - 1) // UNROLL
            for j in range(UNROLL):
                lists[base + early + j] = 0
                lists[span + base + early + j] = total
                lists[2 * span + base + every + j] = 0
                lists[3 * span + base + every + j] = total
        at = late + 2 * LATE * s + behind
        lists[at] = 0
        lists[at + 4 * LATE] = NX * nb
        lists[at + 8 * LATE] = 0


def plan_call(place, col_a, col_b, nb, per):
    smem = pl.BlockSpec(memory_space=pltpu.SMEM)
    return pl.pallas_call(
        functools.partial(plan_kernel, nb=nb, per=per),
        out_shape=jax.ShapeDtypeStruct((plan_offsets(nb)[3],), jnp.int32),
        in_specs=[smem] * 3,
        out_specs=smem,
        name="plan",
    )(place, col_a, col_b)


def transposed_kernel(lists, tiles_a, tiles_b, cot_a, cot_b, *rest):
    outs, (acc, held_a, held_b, sems) = rest[:NX], rest[NX:]
    blk = held_a.shape[1]
    rows = cot_a.shape[0] // blk
    span, counts, _, _ = plan_offsets(rows)
    copy_a = pltpu.make_async_copy(tiles_a, held_a, sems.at[0])
    copy_b = pltpu.make_async_copy(tiles_b, held_b, sems.at[1])
    copy_a.start()
    copy_b.start()
    acc[...] = jnp.zeros_like(acc)
    for s, (copy, tiles, cot) in enumerate(((copy_a, held_a, cot_a), (copy_b, held_b, cot_b))):
        copy.wait()
        for b in range(rows):
            turned = cot[b * blk:(b + 1) * blk, :].T
            base = (s * rows + b) * STRIDE

            def one(i, carry, tiles=tiles, turned=turned, base=base):
                for j in range(UNROLL // 2):
                    at = base + i * UNROLL + 2 * j
                    one_tile, two_tile = lists[2 * span + at], lists[2 * span + at + 1]
                    right = jnp.concatenate([tiles[one_tile], tiles[two_tile]], axis=1)
                    term = jnp.dot(turned, right, preferred_element_type=jnp.float32)
                    one_slot, two_slot = lists[3 * span + at], lists[3 * span + at + 1]
                    acc[one_slot] = acc[one_slot] + term[:, :blk]
                    acc[two_slot] = acc[two_slot] + term[:, blk:]
                return carry

            lax.fori_loop(0, lists[counts + 2 * rows + s * rows + b], one, 0)
    size = outs[0].shape[0]
    for r, out in enumerate(outs):
        out[...] = acc[r * size:(r + 1) * size].astype(out.dtype)


def transposed_terms(lists, tiles_a, tiles_b, cot_a, cot_b, total):
    blk = tiles_a.shape[1]
    width = cot_a.shape[1]
    shape = jax.ShapeDtypeStruct((total // NX, width, blk), jnp.bfloat16)
    smem = pl.BlockSpec(memory_space=pltpu.SMEM)
    vmem = pl.BlockSpec(memory_space=pltpu.VMEM)
    free = pl.BlockSpec(memory_space=pltpu.HBM)
    return pl.pallas_call(
        transposed_kernel,
        out_shape=[shape] * NX,
        in_specs=[smem, free, free, vmem, vmem],
        out_specs=[vmem] * NX,
        scratch_shapes=[
            pltpu.VMEM((total + 1, width, blk), jnp.float32),
            pltpu.VMEM(tiles_a.shape, tiles_a.dtype),
            pltpu.VMEM(tiles_b.shape, tiles_b.dtype),
            pltpu.SemaphoreType.DMA((2,)),
        ],
        compiler_params=pltpu.CompilerParams(vmem_limit_bytes=32 * 1024 * 1024),
        name="transposed_terms",
    )(lists, in_hbm(tiles_a), in_hbm(tiles_b), cot_a, cot_b)


def early_call(lists, tiles_a, tiles_b, pieces, total, rows):
    blk = tiles_a.shape[1]
    width = pieces[0][2].shape[2]
    n = len(pieces)
    span, counts, _, _ = plan_offsets(rows)

    def kernel(lists, tiles_a, tiles_b, *rest):
        parts, (out_a, out_b, held, held_a, held_b, sems) = rest[:n], rest[n:]
        copies = [
            pltpu.make_async_copy(part.at[pl.ds(0, count)], held.at[pl.ds(at, count)], sems.at[i])
            for i, (part, (at, count, _)) in enumerate(zip(parts, pieces))
        ]
        copy_a = pltpu.make_async_copy(tiles_a, held_a, sems.at[n])
        copy_b = pltpu.make_async_copy(tiles_b, held_b, sems.at[n + 1])
        for copy in copies:
            copy.start()
        copy_b.start()
        copy_a.start()
        held[total] = jnp.zeros_like(held[total])
        for copy in copies:
            copy.wait()
        for s, copy, tiles, out in ((1, copy_b, held_b, out_b), (0, copy_a, held_a, out_a)):
            copy.wait()
            for b in range(rows):
                base = (s * rows + b) * STRIDE

                def one(i, summed, tiles=tiles, base=base):
                    for j in range(UNROLL // 2):
                        at = base + i * UNROLL + 2 * j
                        left = jnp.concatenate([tiles[lists[at]], tiles[lists[at + 1]]], axis=1)
                        one_slot, two_slot = lists[span + at], lists[span + at + 1]
                        right = jnp.concatenate([held[one_slot], held[two_slot]], axis=0)
                        summed = summed + jnp.dot(left, right, preferred_element_type=jnp.float32)
                    return summed

                zero = jnp.zeros((blk, width), jnp.float32)
                out[b] = lax.fori_loop(0, lists[counts + s * rows + b], one, zero)

    shape = jax.ShapeDtypeStruct((rows, blk, width), jnp.float32)
    smem = pl.BlockSpec(memory_space=pltpu.SMEM)
    vmem = pl.BlockSpec(memory_space=pltpu.VMEM)
    free = pl.BlockSpec(memory_space=pltpu.HBM)
    return pl.pallas_call(
        kernel,
        out_shape=[shape, shape],
        in_specs=[smem] + [free] * (n + 2),
        out_specs=[vmem, vmem],
        scratch_shapes=[
            pltpu.VMEM((total + 1, blk, width), jnp.bfloat16),
            pltpu.VMEM(tiles_a.shape, tiles_a.dtype),
            pltpu.VMEM(tiles_b.shape, tiles_b.dtype),
            pltpu.SemaphoreType.DMA((n + 2,)),
        ],
        compiler_params=pltpu.CompilerParams(vmem_limit_bytes=24 * 1024 * 1024),
        name="early",
    )(lists, in_hbm(tiles_a), in_hbm(tiles_b), *[in_hbm(part) for _, _, part in pieces])


def late_call(lists, tiles_a, tiles_b, last, early):
    rows, blk, width = early[0].shape
    n = len(last)
    zero = sum(count for _, count, _ in last)
    _, _, late, _ = plan_offsets(rows)

    def kernel(lists, tiles_a, tiles_b, early_a, early_b, *rest):
        parts, (out_a, out_b, held, got, sems) = rest[:n], rest[n:]
        copies = [
            pltpu.make_async_copy(part.at[pl.ds(0, count)], held.at[pl.ds(at, count)], sems.at[i])
            for i, (part, (at, count, _)) in enumerate(zip(parts, last))
        ]
        for s, tiles in ((0, tiles_a), (1, tiles_b)):
            for j in range(LATE):
                at = s * LATE + j
                tile = lists[late + 2 * LATE * s + j]
                copies.append(pltpu.make_async_copy(tiles.at[tile], got.at[at], sems.at[n + at]))
        for copy in copies:
            copy.start()
        held[zero] = jnp.zeros_like(held[zero])
        out_a[...] = early_a[...]
        out_b[...] = early_b[...]
        for copy in copies:
            copy.wait()
        for s, out in ((0, out_a), (1, out_b)):
            for j in range(LATE):
                at = late + 2 * LATE * s + j
                term = jnp.dot(got[s * LATE + j], held[lists[at + 4 * LATE]], preferred_element_type=jnp.float32)
                row = lists[at + 8 * LATE]
                out[row] = out[row] + term

    shape = jax.ShapeDtypeStruct((rows, blk, width), jnp.float32)
    smem = pl.BlockSpec(memory_space=pltpu.SMEM)
    vmem = pl.BlockSpec(memory_space=pltpu.VMEM)
    free = pl.BlockSpec(memory_space=pl.ANY)
    tiled = pl.BlockSpec(memory_space=pltpu.HBM)
    return pl.pallas_call(
        kernel,
        out_shape=[shape, shape],
        in_specs=[smem, tiled, tiled, vmem, vmem] + [free] * n,
        out_specs=[vmem, vmem],
        scratch_shapes=[
            pltpu.VMEM((zero + 1, blk, width), jnp.bfloat16),
            pltpu.VMEM((2 * LATE, blk, blk), tiles_a.dtype),
            pltpu.SemaphoreType.DMA((n + 2 * LATE,)),
        ],
        compiler_params=pltpu.CompilerParams(vmem_limit_bytes=8 * 1024 * 1024),
        name="late",
    )(lists, in_hbm(tiles_a), in_hbm(tiles_b), *early, *[part for _, _, part in last])


def mixing_kernel(place, p0, p1, p2, p3, w_in, w_out, z_out, own_out, mixed_out):
    y = place[3]
    nodes, width = p0.shape
    blk = mixed_out.shape[1]
    for b in range(nodes // blk):
        at = slice(b * blk, (b + 1) * blk)
        z = None
        for r, part in enumerate((p0, p1, p2, p3)):
            row = pl.multiple_of(((y + r) & (NY - 1)) * width, width)
            term = jnp.dot(part[at, :], w_in[pl.ds(row, width), :], preferred_element_type=jnp.float32)
            z = term if z is None else z + term
        z_out[at, :] = z
        hidden = (z * jax.nn.sigmoid(z)).astype(jnp.bfloat16)
        mixed_out[b] = jnp.dot(hidden, w_out[...], preferred_element_type=jnp.float32).astype(jnp.bfloat16)
        own = z_out[at, pl.ds(pl.multiple_of(y * width, width), width)]
        own_out[at, :] = (own * jax.nn.sigmoid(own)).astype(jnp.bfloat16)


def mixing_call(place, parts, w_in, w_out, nb):
    nodes, width = parts[0].shape
    full = w_in.shape[0]
    smem = pl.BlockSpec(memory_space=pltpu.SMEM)
    vmem = pl.BlockSpec(memory_space=pltpu.VMEM)
    return pl.pallas_call(
        mixing_kernel,
        out_shape=[
            jax.ShapeDtypeStruct((nodes, full), jnp.float32),
            jax.ShapeDtypeStruct((nodes, width), jnp.bfloat16),
            jax.ShapeDtypeStruct((nb, nodes // nb, width), jnp.bfloat16),
        ],
        in_specs=[smem] + [vmem] * (NY + 2),
        out_specs=[vmem] * 3,
        compiler_params=pltpu.CompilerParams(vmem_limit_bytes=16 * 1024 * 1024),
        name="mixing",
    )(place, *parts, w_in, w_out)


def grads_kernel(place, z_all, prop, own, q0, q1, q2, q3, w_two, keep, give, both, *, factor):
    y = place[3]
    nodes, width = prop.shape
    blk = 128 if nodes % 128 == 0 else nodes
    down = (((0,), (0,)), ((), ()))
    across = (((1,), (1,)), ((), ()))
    first = None
    second = [None] * NY
    for b in range(nodes // blk):
        at = slice(b * blk, (b + 1) * blk)
        hidden_grad = None
        for r, part in enumerate((q0, q1, q2, q3)):
            col = pl.multiple_of(((y + r) & (NY - 1)) * width, width)
            term = lax.dot_general(part[at, :], w_two[:, pl.ds(col, width)], across, preferred_element_type=jnp.float32)
            hidden_grad = term if hidden_grad is None else hidden_grad + term
            term = lax.dot_general(own[at, :], part[at, :], down, preferred_element_type=jnp.float32)
            second[r] = term if second[r] is None else second[r] + term
        z = z_all[at, :]
        sigma = jax.nn.sigmoid(z)
        grad_z = (hidden_grad * sigma * (1.0 + z * (1.0 - sigma))).astype(jnp.bfloat16)
        term = lax.dot_general(prop[at, :], grad_z, down, preferred_element_type=jnp.float32)
        first = term if first is None else first + term
    both[0] = first * factor
    for r in range(NY):
        col = pl.multiple_of(((y + r) & (NY - 1)) * width, width)
        both[1, :, pl.ds(col, width)] = second[r] * factor
    mine = place[2]
    for r in range(NY):
        cols = slice(r * width, (r + 1) * width)
        rows = slice(r * width, (r + 1) * width)
        keep[rows, :] = both[mine, :, cols]
        give[rows, :] = both[1 - mine, :, cols]


def grads_call(place, z_all, prop, own, parts, w_two, factor):
    width = prop.shape[1]
    full = w_two.shape[0]
    smem = pl.BlockSpec(memory_space=pltpu.SMEM)
    vmem = pl.BlockSpec(memory_space=pltpu.VMEM)
    return pl.pallas_call(
        functools.partial(grads_kernel, factor=factor),
        out_shape=[jax.ShapeDtypeStruct((full, width), jnp.float32)] * 2,
        in_specs=[smem] + [vmem] * (NY + 4),
        out_specs=[vmem] * 2,
        scratch_shapes=[pltpu.VMEM((2, width, full), jnp.float32)],
        compiler_params=pltpu.CompilerParams(vmem_limit_bytes=16 * 1024 * 1024),
        name="grads",
    )(place, z_all, prop, own, *parts, w_two)


def step(node_feats, weight_one, weight_two, adj_tiles, tile_owner, tile_local, cotangent):
    nb, per, blk, _ = adj_tiles.shape
    nodes, width = node_feats.shape
    full = weight_one.shape[0]
    node_count = NX * NZ * NC
    index = lax.axis_index("nodes")
    y = lax.axis_index("feat")
    place = jnp.stack([index // (NZ * NC), (index // NC) % NZ, index % NC, y]).astype(jnp.int32)
    bf = jnp.bfloat16
    total = NX * NZ * nb

    tiles = adj_tiles.reshape(nb * per, blk, blk)
    column = (tile_owner * nb + tile_local)[:, 0]
    column_other = send(column, dc=1)
    tiles_other = send(tiles, dc=1)
    cot_other = send(cotangent, dc=1)
    lists = plan_call(place, column, column_other, nb, per)

    def spread(features, extra=None):
        near, last, extras = gather_plane(features, extra)
        early = early_call(lists, tiles, tiles_other, near, total, nb)
        mine, theirs = late_call(lists, tiles, tiles_other, last, early)
        return (mine + send(theirs, dc=1)).reshape(nodes, width).astype(bf), extras

    terms = transposed_terms(lists, tiles, tiles_other, cotangent, cot_other, total)
    turned = jnp.swapaxes(reduce_plane(terms, nb), 1, 2).reshape(nodes, width).astype(bf)

    weight_out = lax.dynamic_slice_in_dim(weight_two, y * width, width, 1)
    prop_one, _ = spread(node_feats.reshape(nb, blk, width))
    prop_parts = gather_y(prop_one)
    z_one, hidden_own, mixed = mixing_call(place, prop_parts, weight_one, weight_out, nb)

    turned_parts = gather_y(turned)
    factor = 1.0 / math.sqrt(nodes * node_count)
    both = grads_call(place, z_one, prop_one, hidden_own, turned_parts, weight_two, factor)
    part = halve(both, index)
    high = part.astype(bf)
    low = (part - high.astype(jnp.float32)).astype(bf)
    layer_output, extras = spread(mixed, jnp.stack([high, low]))
    for extra in extras:
        part = part + extra[0].astype(jnp.float32) + extra[1].astype(jnp.float32)
    summed = double(part, index).reshape(2, NY, width, width)
    summed = jnp.swapaxes(summed, 1, 2).reshape(2, width, full)
    return (layer_output, summed[0], summed[1])


def solution(mesh):
    placed = (
        P("nodes", "feat"),
        P(),
        P(),
        P("nodes", None, None, None),
        P("nodes", None),
        P("nodes", None),
        P("nodes", "feat"),
    )
    return jax.shard_map(
        step,
        mesh=mesh,
        in_specs=placed,
        out_specs=(P("nodes", "feat"), P("feat", None), P("feat", None)),
        check_vma=False,
    )
```

```python
import functools
import math

import jax
import jax.numpy as jnp
from jax import lax
from jax.experimental import pallas as pl
from jax.experimental.pallas import tpu as pltpu
from jax.sharding import PartitionSpec as P


NX, NZ, NC, NY = 4, 8, 2, 4


STRIDE = 32
UNROLL = 6
LATE = 8


def node_pairs(dx, dz, dc):
    pairs = []
    for x in range(NX):
        for z in range(NZ):
            for c in range(NC):
                there = (((x + dx) % NX) * NZ + (z + dz) % NZ) * NC + (c + dc) % NC
                pairs.append(((x * NZ + z) * NC + c, there))
    return pairs


def xor_pairs(bit):
    return [(i, i ^ bit) for i in range(NX * NZ * NC)]


def in_hbm(value):
    return pltpu.with_memory_space_constraint(value, pltpu.HBM)


def send(value, dx=0, dz=0, dc=0):
    return lax.ppermute(value, "nodes", node_pairs(dx, dz, dc))


def gather_y(value):
    pairs = [[(y, (y - r) % NY) for y in range(NY)] for r in range(NY)]
    return [value] + [lax.ppermute(value, "feat", pairs[r]) for r in range(1, NY)]


def ring_z(block):
    half = block.shape[0] // 2
    low, high = [block], [block]
    for _ in range(1, 4):
        low.append(send(low[-1], dz=1))
        high.append(send(high[-1], dz=-1))
    first = send(low[3][:half], dz=1)
    second = send(high[3][half:], dz=-1)
    return [block, high[1], high[2], high[3], (first, second), low[3], low[2], low[1]]


def gather_plane(own):
    nb = own.shape[0]
    beside = [send(own, dx=-r) for r in (1, 2, 3)]
    near, last = [], []
    for r, entry in enumerate(ring_z(join_call([own] + beside))):
        if r == NZ // 2:
            half = entry[0].shape[0]
            last = [(0, half, entry[0]), (half, half, entry[1])]
        else:
            near.append((r * NX * nb, NX * nb, entry))
    return near, last


def join_call(parts):
    size, blk, width = parts[0].shape
    n = len(parts)

    def kernel(*refs):
        for i in range(n):
            refs[n][i * size:(i + 1) * size] = refs[i][...]

    vmem = pl.BlockSpec(memory_space=pltpu.VMEM)
    return pl.pallas_call(
        kernel,
        out_shape=jax.ShapeDtypeStruct((n * size, blk, width), parts[0].dtype),
        in_specs=[vmem] * n,
        out_specs=vmem,
        compiler_params=pltpu.CompilerParams(vmem_limit_bytes=4 * 1024 * 1024),
        name="join",
    )(*parts)


def reduce_plane(parts, nb):
    f32, bf = jnp.float32, jnp.bfloat16
    half = NZ * nb // 2
    far = parts[2]
    up_far = send(far[:half], dx=1)
    down_far = send(far[half:], dx=-1)
    up_sum = (parts[1][:half].astype(f32) + up_far.astype(f32)).astype(bf)
    down_sum = (parts[3][half:].astype(f32) + down_far.astype(f32)).astype(bf)
    up = lax.dynamic_update_slice(parts[1], up_sum, (0, 0, 0))
    down = lax.dynamic_update_slice(parts[3], down_sum, (half, 0, 0))
    own = parts[0].astype(f32) + send(up, dx=1).astype(f32) + send(down, dx=-1).astype(f32)
    for bit in (1, 2, 4):
        half = own.shape[0] // 2
        give = own[half:].astype(bf)
        own = own[:half] + lax.ppermute(give, "nodes", xor_pairs(bit * NC)).astype(f32)
    return own


def halve(value, index):
    value, give = value
    value = value + lax.ppermute(give, "nodes", xor_pairs(1))
    for bit in (16, 32):
        half = value.shape[0] // 2
        upper = (index & bit) != 0
        mine = jnp.where(upper, value[half:], value[:half])
        give = jnp.where(upper, value[:half], value[half:])
        value = mine + lax.ppermute(give, "nodes", xor_pairs(bit))
    for bit in (2, 4, 8):
        value = value + lax.ppermute(value, "nodes", xor_pairs(bit))
    return value


def double(value, index):
    for bit in (32, 16, 1):
        upper = (index & bit) != 0
        other = lax.ppermute(value, "nodes", xor_pairs(bit))
        value = jnp.concatenate([jnp.where(upper, other, value), jnp.where(upper, value, other)], axis=0)
    return value


def plan_offsets(nb):
    span = 2 * nb * STRIDE
    counts = 4 * span
    late = counts + 4 * nb
    return span, counts, late, late + 8 * LATE * 3


def plan_kernel(place, col_a, col_b, lists, *, nb, per):
    bits = nb.bit_length() - 1
    x, z, c = place[0], place[1], place[2]
    total = NX * NZ * nb
    span, counts, late, _ = plan_offsets(nb)
    for j in range(4 * LATE):
        lists[late + j] = 0
        lists[late + 4 * LATE + j] = NX * nb
        lists[late + 8 * LATE + j] = 0
    for s, cols in enumerate((col_a, col_b)):
        behind = 0
        for b in range(nb):
            base = (s * nb + b) * STRIDE

            def one(k, carry, cols=cols, b=b, base=base, s=s):
                early, every, behind = carry
                column = cols[b * per + k]
                local = column & (nb - 1)
                owner = column >> bits
                rx = ((owner >> 4) - x) & (NX - 1)
                zo = (owner >> 1) & (NZ - 1)
                rz = (zo - z) & (NZ - 1)
                rel = zo ^ z
                rank = ((rel & 1) << 2) | (rel & 2) | (rel >> 2)
                mine = jnp.where((owner & 1) == c, 1, 0)
                far = jnp.where(rz == NZ // 2, mine, 0)
                lists[base + early] = b * per + k
                lists[span + base + early] = (rz * NX + rx) * nb + local
                lists[2 * span + base + every] = b * per + k
                lists[3 * span + base + every] = (rx * NZ + rank) * nb + local
                at = late + 2 * LATE * s + behind
                lists[at] = b * per + k
                lists[at + 4 * LATE] = rx * nb + local
                lists[at + 8 * LATE] = b
                return early + mine - far, every + mine, behind + far

            early, every, behind = lax.fori_loop(0, per, one, (0, 0, behind), unroll=2)
            lists[counts + s * nb + b] = (early + UNROLL - 1) // UNROLL
            lists[counts + 2 * nb + s * nb + b] = (every + UNROLL - 1) // UNROLL
            for j in range(UNROLL):
                lists[base + early + j] = 0
                lists[span + base + early + j] = total
                lists[2 * span + base + every + j] = 0
                lists[3 * span + base + every + j] = total
        at = late + 2 * LATE * s + behind
        lists[at] = 0
        lists[at + 4 * LATE] = NX * nb
        lists[at + 8 * LATE] = 0


def plan_call(place, col_a, col_b, nb, per):
    smem = pl.BlockSpec(memory_space=pltpu.SMEM)
    return pl.pallas_call(
        functools.partial(plan_kernel, nb=nb, per=per),
        out_shape=jax.ShapeDtypeStruct((plan_offsets(nb)[3],), jnp.int32),
        in_specs=[smem] * 3,
        out_specs=smem,
        name="plan",
    )(place, col_a, col_b)


def transposed_kernel(lists, tiles_a, tiles_b, cot_a, cot_b, *rest):
    outs, (acc, held_a, held_b, sems) = rest[:NX], rest[NX:]
    blk = held_a.shape[1]
    rows = cot_a.shape[0] // blk
    span, counts, _, _ = plan_offsets(rows)
    copy_a = pltpu.make_async_copy(tiles_a, held_a, sems.at[0])
    copy_b = pltpu.make_async_copy(tiles_b, held_b, sems.at[1])
    copy_a.start()
    copy_b.start()
    acc[...] = jnp.zeros_like(acc)
    for s, (copy, tiles, cot) in enumerate(((copy_a, held_a, cot_a), (copy_b, held_b, cot_b))):
        copy.wait()

        def block(b, carry, s=s, tiles=tiles, cot=cot):
            turned = cot[pl.ds(pl.multiple_of(b * blk, blk), blk), :].T
            base = (s * rows + b) * STRIDE

            def one(i, carry):
                for j in range(UNROLL // 2):
                    at = base + i * UNROLL + 2 * j
                    one_tile, two_tile = lists[2 * span + at], lists[2 * span + at + 1]
                    right = jnp.concatenate([tiles[one_tile], tiles[two_tile]], axis=1)
                    term = jnp.dot(turned, right, preferred_element_type=jnp.float32)
                    one_slot, two_slot = lists[3 * span + at], lists[3 * span + at + 1]
                    acc[one_slot] = acc[one_slot] + term[:, :blk]
                    acc[two_slot] = acc[two_slot] + term[:, blk:]
                return carry

            return lax.fori_loop(0, lists[counts + 2 * rows + s * rows + b], one, carry)

        lax.fori_loop(0, rows, block, 0)
    size = outs[0].shape[0]
    for r, out in enumerate(outs):
        out[...] = acc[r * size:(r + 1) * size].astype(out.dtype)


def transposed_terms(lists, tiles_a, tiles_b, cot_a, cot_b, total):
    blk = tiles_a.shape[1]
    width = cot_a.shape[1]
    shape = jax.ShapeDtypeStruct((total // NX, width, blk), jnp.bfloat16)
    smem = pl.BlockSpec(memory_space=pltpu.SMEM)
    vmem = pl.BlockSpec(memory_space=pltpu.VMEM)
    free = pl.BlockSpec(memory_space=pltpu.HBM)
    return pl.pallas_call(
        transposed_kernel,
        out_shape=[shape] * NX,
        in_specs=[smem, free, free, vmem, vmem],
        out_specs=[vmem] * NX,
        scratch_shapes=[
            pltpu.VMEM((total + 1, width, blk), jnp.float32),
            pltpu.VMEM(tiles_a.shape, tiles_a.dtype),
            pltpu.VMEM(tiles_b.shape, tiles_b.dtype),
            pltpu.SemaphoreType.DMA((2,)),
        ],
        compiler_params=pltpu.CompilerParams(vmem_limit_bytes=32 * 1024 * 1024),
        name="transposed_terms",
    )(lists, in_hbm(tiles_a), in_hbm(tiles_b), cot_a, cot_b)


def early_call(lists, tiles_a, tiles_b, pieces, total, rows):
    blk = tiles_a.shape[1]
    width = pieces[0][2].shape[2]
    n = len(pieces)
    span, counts, _, _ = plan_offsets(rows)

    def kernel(lists, tiles_a, tiles_b, *rest):
        parts, (out_a, out_b, held, held_a, held_b, sems) = rest[:n], rest[n:]
        copies = [
            pltpu.make_async_copy(part.at[pl.ds(0, count)], held.at[pl.ds(at, count)], sems.at[i])
            for i, (part, (at, count, _)) in enumerate(zip(parts, pieces))
        ]
        copy_a = pltpu.make_async_copy(tiles_a, held_a, sems.at[n])
        copy_b = pltpu.make_async_copy(tiles_b, held_b, sems.at[n + 1])
        for copy in copies:
            copy.start()
        copy_b.start()
        copy_a.start()
        held[total] = jnp.zeros_like(held[total])
        for copy in copies:
            copy.wait()
        for s, copy, tiles, out in ((1, copy_b, held_b, out_b), (0, copy_a, held_a, out_a)):
            copy.wait()

            def block(b, carry, s=s, tiles=tiles, out=out):
                base = (s * rows + b) * STRIDE

                def one(i, summed):
                    for j in range(UNROLL // 2):
                        at = base + i * UNROLL + 2 * j
                        left = jnp.concatenate([tiles[lists[at]], tiles[lists[at + 1]]], axis=1)
                        one_slot, two_slot = lists[span + at], lists[span + at + 1]
                        right = jnp.concatenate([held[one_slot], held[two_slot]], axis=0)
                        summed = summed + jnp.dot(left, right, preferred_element_type=jnp.float32)
                    return summed

                zero = jnp.zeros((blk, width), jnp.float32)
                out[b] = lax.fori_loop(0, lists[counts + s * rows + b], one, zero)
                return carry

            lax.fori_loop(0, rows, block, 0)

    shape = jax.ShapeDtypeStruct((rows, blk, width), jnp.float32)
    smem = pl.BlockSpec(memory_space=pltpu.SMEM)
    vmem = pl.BlockSpec(memory_space=pltpu.VMEM)
    free = pl.BlockSpec(memory_space=pltpu.HBM)
    return pl.pallas_call(
        kernel,
        out_shape=[shape, shape],
        in_specs=[smem] + [free] * (n + 2),
        out_specs=[vmem, vmem],
        scratch_shapes=[
            pltpu.VMEM((total + 1, blk, width), jnp.bfloat16),
            pltpu.VMEM(tiles_a.shape, tiles_a.dtype),
            pltpu.VMEM(tiles_b.shape, tiles_b.dtype),
            pltpu.SemaphoreType.DMA((n + 2,)),
        ],
        compiler_params=pltpu.CompilerParams(vmem_limit_bytes=24 * 1024 * 1024),
        name="early",
    )(lists, in_hbm(tiles_a), in_hbm(tiles_b), *[in_hbm(part) for _, _, part in pieces])


def late_call(lists, tiles_a, tiles_b, last, early):
    rows, blk, width = early[0].shape
    n = len(last)
    zero = sum(count for _, count, _ in last)
    _, _, late, _ = plan_offsets(rows)

    def kernel(lists, tiles_a, tiles_b, early_a, early_b, *rest):
        parts, (out_a, out_b, held, got, sems) = rest[:n], rest[n:]
        copies = [
            pltpu.make_async_copy(part.at[pl.ds(0, count)], held.at[pl.ds(at, count)], sems.at[i])
            for i, (part, (at, count, _)) in enumerate(zip(parts, last))
        ]
        for s, tiles in ((0, tiles_a), (1, tiles_b)):
            for j in range(LATE):
                at = s * LATE + j
                tile = lists[late + 2 * LATE * s + j]
                copies.append(pltpu.make_async_copy(tiles.at[tile], got.at[at], sems.at[n + at]))
        for copy in copies:
            copy.start()
        held[zero] = jnp.zeros_like(held[zero])
        out_a[...] = early_a[...]
        out_b[...] = early_b[...]
        for copy in copies:
            copy.wait()
        for s, out in ((0, out_a), (1, out_b)):

            def some(i, carry, s=s, out=out):
                for j in range(LATE // 2):
                    k = i * (LATE // 2) + j
                    at = late + 2 * LATE * s + k
                    term = jnp.dot(got[s * LATE + k], held[lists[at + 4 * LATE]], preferred_element_type=jnp.float32)
                    row = lists[at + 8 * LATE]
                    out[row] = out[row] + term
                return carry

            lax.fori_loop(0, 2, some, 0)

    shape = jax.ShapeDtypeStruct((rows, blk, width), jnp.float32)
    smem = pl.BlockSpec(memory_space=pltpu.SMEM)
    vmem = pl.BlockSpec(memory_space=pltpu.VMEM)
    free = pl.BlockSpec(memory_space=pl.ANY)
    tiled = pl.BlockSpec(memory_space=pltpu.HBM)
    return pl.pallas_call(
        kernel,
        out_shape=[shape, shape],
        in_specs=[smem, tiled, tiled, vmem, vmem] + [free] * n,
        out_specs=[vmem, vmem],
        scratch_shapes=[
            pltpu.VMEM((zero + 1, blk, width), jnp.bfloat16),
            pltpu.VMEM((2 * LATE, blk, blk), tiles_a.dtype),
            pltpu.SemaphoreType.DMA((n + 2 * LATE,)),
        ],
        compiler_params=pltpu.CompilerParams(vmem_limit_bytes=8 * 1024 * 1024),
        name="late",
    )(lists, in_hbm(tiles_a), in_hbm(tiles_b), *early, *[part for _, _, part in last])


def mixing_kernel(place, p0, p1, p2, p3, w_in, w_out, z_out, own_out, mixed_out):
    y = place[3]
    nodes, width = p0.shape
    blk = mixed_out.shape[1]

    def block(b, carry):
        at = pl.ds(pl.multiple_of(b * blk, blk), blk)
        z = None
        for r, part in enumerate((p0, p1, p2, p3)):
            row = pl.multiple_of(((y + r) & (NY - 1)) * width, width)
            term = jnp.dot(part[at, :], w_in[pl.ds(row, width), :], preferred_element_type=jnp.float32)
            z = term if z is None else z + term
        z_out[at, :] = z
        hidden = (z * jax.nn.sigmoid(z)).astype(jnp.bfloat16)
        mixed_out[b] = jnp.dot(hidden, w_out[...], preferred_element_type=jnp.float32).astype(jnp.bfloat16)
        own = z_out[at, pl.ds(pl.multiple_of(y * width, width), width)]
        own_out[at, :] = (own * jax.nn.sigmoid(own)).astype(jnp.bfloat16)
        return carry

    lax.fori_loop(0, nodes // blk, block, 0)


def mixing_call(place, parts, w_in, w_out, nb):
    nodes, width = parts[0].shape
    full = w_in.shape[0]
    smem = pl.BlockSpec(memory_space=pltpu.SMEM)
    vmem = pl.BlockSpec(memory_space=pltpu.VMEM)
    return pl.pallas_call(
        mixing_kernel,
        out_shape=[
            jax.ShapeDtypeStruct((nodes, full), jnp.float32),
            jax.ShapeDtypeStruct((nodes, width), jnp.bfloat16),
            jax.ShapeDtypeStruct((nb, nodes // nb, width), jnp.bfloat16),
        ],
        in_specs=[smem] + [vmem] * (NY + 2),
        out_specs=[vmem] * 3,
        compiler_params=pltpu.CompilerParams(vmem_limit_bytes=16 * 1024 * 1024),
        name="mixing",
    )(place, *parts, w_in, w_out)


def grads_kernel(place, z_all, prop, own, q0, q1, q2, q3, w_two, keep, give, both, *, factor):
    y = place[3]
    nodes, width = prop.shape
    blk = 128 if nodes % 128 == 0 else nodes
    down = (((0,), (0,)), ((), ()))
    across = (((1,), (1,)), ((), ()))
    both[...] = jnp.zeros_like(both)

    def block(b, carry):
        at = pl.ds(pl.multiple_of(b * blk, blk), blk)
        hidden_grad = None
        for r, part in enumerate((q0, q1, q2, q3)):
            col = pl.multiple_of(((y + r) & (NY - 1)) * width, width)
            term = lax.dot_general(part[at, :], w_two[:, pl.ds(col, width)], across, preferred_element_type=jnp.float32)
            hidden_grad = term if hidden_grad is None else hidden_grad + term
            term = lax.dot_general(own[at, :], part[at, :], down, preferred_element_type=jnp.float32)
            both[1, :, pl.ds(col, width)] = both[1, :, pl.ds(col, width)] + term * factor
        z = z_all[at, :]
        sigma = jax.nn.sigmoid(z)
        grad_z = (hidden_grad * sigma * (1.0 + z * (1.0 - sigma))).astype(jnp.bfloat16)
        term = lax.dot_general(prop[at, :], grad_z, down, preferred_element_type=jnp.float32)
        both[0] = both[0] + term * factor
        return carry

    lax.fori_loop(0, nodes // blk, block, 0)
    mine = place[2]
    for r in range(NY):
        cols = slice(r * width, (r + 1) * width)
        rows = slice(r * width, (r + 1) * width)
        keep[rows, :] = both[mine, :, cols]
        give[rows, :] = both[1 - mine, :, cols]


def grads_call(place, z_all, prop, own, parts, w_two, factor):
    width = prop.shape[1]
    full = w_two.shape[0]
    smem = pl.BlockSpec(memory_space=pltpu.SMEM)
    vmem = pl.BlockSpec(memory_space=pltpu.VMEM)
    return pl.pallas_call(
        functools.partial(grads_kernel, factor=factor),
        out_shape=[jax.ShapeDtypeStruct((full, width), jnp.float32)] * 2,
        in_specs=[smem] + [vmem] * (NY + 4),
        out_specs=[vmem] * 2,
        scratch_shapes=[pltpu.VMEM((2, width, full), jnp.float32)],
        compiler_params=pltpu.CompilerParams(vmem_limit_bytes=16 * 1024 * 1024),
        name="grads",
    )(place, z_all, prop, own, *parts, w_two)


def step(node_feats, weight_one, weight_two, adj_tiles, tile_owner, tile_local, cotangent):
    nb, per, blk, _ = adj_tiles.shape
    nodes, width = node_feats.shape
    full = weight_one.shape[0]
    node_count = NX * NZ * NC
    index = lax.axis_index("nodes")
    y = lax.axis_index("feat")
    place = jnp.stack([index // (NZ * NC), (index // NC) % NZ, index % NC, y]).astype(jnp.int32)
    bf = jnp.bfloat16
    total = NX * NZ * nb

    tiles = adj_tiles.reshape(nb * per, blk, blk)
    column = (tile_owner * nb + tile_local)[:, 0]
    column_other = send(column, dc=1)
    tiles_other = send(tiles, dc=1)
    cot_other = send(cotangent, dc=1)
    lists = plan_call(place, column, column_other, nb, per)

    def spread(features):
        near, last = gather_plane(features)
        early = early_call(lists, tiles, tiles_other, near, total, nb)
        mine, theirs = late_call(lists, tiles, tiles_other, last, early)
        return (mine + send(theirs, dc=1)).reshape(nodes, width).astype(bf)

    terms = transposed_terms(lists, tiles, tiles_other, cotangent, cot_other, total)
    turned = jnp.swapaxes(reduce_plane(terms, nb), 1, 2).reshape(nodes, width).astype(bf)

    weight_out = lax.dynamic_slice_in_dim(weight_two, y * width, width, 1)
    prop_one = spread(node_feats.reshape(nb, blk, width))
    prop_parts = gather_y(prop_one)
    z_one, hidden_own, mixed = mixing_call(place, prop_parts, weight_one, weight_out, nb)

    turned_parts = gather_y(turned)
    factor = 1.0 / math.sqrt(nodes * node_count)
    both = grads_call(place, z_one, prop_one, hidden_own, turned_parts, weight_two, factor)
    part = halve(both, index)
    layer_output = spread(mixed)
    summed = double(part, index).reshape(2, NY, width, width)
    summed = jnp.swapaxes(summed, 1, 2).reshape(2, width, full)
    return (layer_output, summed[0], summed[1])


def solution(mesh):
    placed = (
        P("nodes", "feat"),
        P(),
        P(),
        P("nodes", None, None, None),
        P("nodes", None),
        P("nodes", None),
        P("nodes", "feat"),
    )
    return jax.shard_map(
        step,
        mesh=mesh,
        in_specs=placed,
        out_specs=(P("nodes", "feat"), P("feat", None), P("feat", None)),
        check_vma=False,
    )
```

```python
import functools
import math

import jax
import jax.numpy as jnp
from jax import lax
from jax.experimental import pallas as pl
from jax.experimental.pallas import tpu as pltpu
from jax.sharding import PartitionSpec as P


NX, NZ, NC, NY = 4, 8, 2, 4


STRIDE = 32
UNROLL = 6
LATE = 8


def node_pairs(dx, dz, dc):
    pairs = []
    for x in range(NX):
        for z in range(NZ):
            for c in range(NC):
                there = (((x + dx) % NX) * NZ + (z + dz) % NZ) * NC + (c + dc) % NC
                pairs.append(((x * NZ + z) * NC + c, there))
    return pairs


def xor_pairs(bit):
    return [(i, i ^ bit) for i in range(NX * NZ * NC)]


def in_hbm(value):
    return pltpu.with_memory_space_constraint(value, pltpu.HBM)


def send(value, dx=0, dz=0, dc=0):
    return lax.ppermute(value, "nodes", node_pairs(dx, dz, dc))


def gather_y(value):
    pairs = [[(y, (y - r) % NY) for y in range(NY)] for r in range(NY)]
    return [value] + [lax.ppermute(value, "feat", pairs[r]) for r in range(1, NY)]


def ring_z(block):
    half = block.shape[0] // 2
    low, high = [block], [block]
    for _ in range(1, 4):
        low.append(send(low[-1], dz=1))
        high.append(send(high[-1], dz=-1))
    first = send(low[3][:half], dz=1)
    second = send(high[3][half:], dz=-1)
    return [block, high[1], high[2], high[3], (first, second), low[3], low[2], low[1]]


def gather_plane(own):
    nb = own.shape[0]
    beside = [send(own, dx=-r) for r in (1, 2, 3)]
    near, last = [], []
    for r, entry in enumerate(ring_z(join_call([own] + beside))):
        if r == NZ // 2:
            half = entry[0].shape[0]
            last = [(0, half, entry[0]), (half, half, entry[1])]
        else:
            near.append((r * NX * nb, NX * nb, entry))
    return near, last


def join_call(parts):
    size, blk, width = parts[0].shape
    n = len(parts)

    def kernel(*refs):
        for i in range(n):
            refs[n][i * size:(i + 1) * size] = refs[i][...]

    vmem = pl.BlockSpec(memory_space=pltpu.VMEM)
    return pl.pallas_call(
        kernel,
        out_shape=jax.ShapeDtypeStruct((n * size, blk, width), parts[0].dtype),
        in_specs=[vmem] * n,
        out_specs=vmem,
        compiler_params=pltpu.CompilerParams(vmem_limit_bytes=4 * 1024 * 1024),
        name="join",
    )(*parts)


def fold_kernel(p1, p3, up_far, down_far, up, down):
    half = up_far.shape[0]
    f32 = jnp.float32

    def one(i, carry):
        up[i] = (p1[i].astype(f32) + up_far[i].astype(f32)).astype(up.dtype)
        up[half + i] = p1[half + i]
        down[i] = p3[i]
        down[half + i] = (p3[half + i].astype(f32) + down_far[i].astype(f32)).astype(down.dtype)
        return carry

    lax.fori_loop(0, half, one, 0)


def fold_call(p1, p3, up_far, down_far):
    vmem = pl.BlockSpec(memory_space=pltpu.VMEM)
    return pl.pallas_call(
        fold_kernel,
        out_shape=[jax.ShapeDtypeStruct(p1.shape, p1.dtype)] * 2,
        in_specs=[vmem] * 4,
        out_specs=[vmem] * 2,
        compiler_params=pltpu.CompilerParams(vmem_limit_bytes=8 * 1024 * 1024),
        name="fold",
    )(p1, p3, up_far, down_far)


def sum_kernel(p0, up, down, keep, give):
    half = keep.shape[0]
    f32 = jnp.float32

    def one(i, carry):
        keep[i] = p0[i].astype(f32) + up[i].astype(f32) + down[i].astype(f32)
        far = half + i
        give[i] = (p0[far].astype(f32) + up[far].astype(f32) + down[far].astype(f32)).astype(give.dtype)
        return carry

    lax.fori_loop(0, half, one, 0)


def sum_call(p0, up, down):
    vmem = pl.BlockSpec(memory_space=pltpu.VMEM)
    size, width, blk = p0.shape
    return pl.pallas_call(
        sum_kernel,
        out_shape=[
            jax.ShapeDtypeStruct((size // 2, width, blk), jnp.float32),
            jax.ShapeDtypeStruct((size // 2, width, blk), p0.dtype),
        ],
        in_specs=[vmem] * 3,
        out_specs=[vmem] * 2,
        compiler_params=pltpu.CompilerParams(vmem_limit_bytes=8 * 1024 * 1024),
        name="sum",
    )(p0, up, down)


def reduce_plane(parts, nb):
    f32, bf = jnp.float32, jnp.bfloat16
    half = NZ * nb // 2
    far = parts[2]
    up_far = send(far[:half], dx=1)
    down_far = send(far[half:], dx=-1)
    up, down = fold_call(parts[1], parts[3], up_far, down_far)
    own, give = sum_call(parts[0], send(up, dx=1), send(down, dx=-1))
    own = own + lax.ppermute(give, "nodes", xor_pairs(NC)).astype(f32)
    for bit in (2, 4):
        half = own.shape[0] // 2
        give = own[half:].astype(bf)
        own = own[:half] + lax.ppermute(give, "nodes", xor_pairs(bit * NC)).astype(f32)
    return own


def halve(value, index):
    value, give = value
    value = value + lax.ppermute(give, "nodes", xor_pairs(1))
    for bit in (16,):
        half = value.shape[0] // 2
        upper = (index & bit) != 0
        mine = jnp.where(upper, value[half:], value[:half])
        give = jnp.where(upper, value[:half], value[half:])
        value = mine + lax.ppermute(give, "nodes", xor_pairs(bit))
    for bit in (32, 2, 4, 8):
        value = value + lax.ppermute(value, "nodes", xor_pairs(bit))
    return value


def double(value, index):
    for bit in (16, 1):
        upper = (index & bit) != 0
        other = lax.ppermute(value, "nodes", xor_pairs(bit))
        value = jnp.concatenate([jnp.where(upper, other, value), jnp.where(upper, value, other)], axis=0)
    return value


def plan_offsets(nb):
    span = 2 * nb * STRIDE
    counts = 4 * span
    late = counts + 4 * nb
    return span, counts, late, late + 8 * LATE * 3


def plan_kernel(place, col_a, col_b, lists, *, nb, per):
    bits = nb.bit_length() - 1
    x, z, c = place[0], place[1], place[2]
    total = NX * NZ * nb
    span, counts, late, _ = plan_offsets(nb)
    for j in range(4 * LATE):
        lists[late + j] = 0
        lists[late + 4 * LATE + j] = NX * nb
        lists[late + 8 * LATE + j] = 0
    for s, cols in enumerate((col_a, col_b)):

        def block(b, behind, cols=cols, s=s):
            base = (s * nb + b) * STRIDE

            def one(k, carry):
                early, every, behind = carry
                column = cols[b * per + k]
                local = column & (nb - 1)
                owner = column >> bits
                rx = ((owner >> 4) - x) & (NX - 1)
                zo = (owner >> 1) & (NZ - 1)
                rz = (zo - z) & (NZ - 1)
                rel = zo ^ z
                rank = ((rel & 1) << 2) | (rel & 2) | (rel >> 2)
                mine = jnp.where((owner & 1) == c, 1, 0)
                far = jnp.where(rz == NZ // 2, mine, 0)
                lists[base + early] = b * per + k
                lists[span + base + early] = (rz * NX + rx) * nb + local
                lists[2 * span + base + every] = b * per + k
                lists[3 * span + base + every] = (rx * NZ + rank) * nb + local
                at = late + 2 * LATE * s + behind
                lists[at] = b * per + k
                lists[at + 4 * LATE] = rx * nb + local
                lists[at + 8 * LATE] = b
                return early + mine - far, every + mine, behind + far

            early, every, behind = lax.fori_loop(0, per, one, (0, 0, behind))
            lists[counts + s * nb + b] = (early + UNROLL - 1) // UNROLL
            lists[counts + 2 * nb + s * nb + b] = (every + UNROLL - 1) // UNROLL
            for j in range(UNROLL):
                lists[base + early + j] = 0
                lists[span + base + early + j] = total
                lists[2 * span + base + every + j] = 0
                lists[3 * span + base + every + j] = total
            return behind

        behind = lax.fori_loop(0, nb, block, 0)
        at = late + 2 * LATE * s + behind
        lists[at] = 0
        lists[at + 4 * LATE] = NX * nb
        lists[at + 8 * LATE] = 0


def plan_call(place, col_a, col_b, nb, per):
    smem = pl.BlockSpec(memory_space=pltpu.SMEM)
    return pl.pallas_call(
        functools.partial(plan_kernel, nb=nb, per=per),
        out_shape=jax.ShapeDtypeStruct((plan_offsets(nb)[3],), jnp.int32),
        in_specs=[smem] * 3,
        out_specs=smem,
        name="plan",
    )(place, col_a, col_b)


def transposed_kernel(lists, tiles_a, tiles_b, cot_a, cot_b, *rest):
    outs, (acc, held_a, held_b, sems) = rest[:NX], rest[NX:]
    blk = held_a.shape[1]
    rows = cot_a.shape[0] // blk
    span, counts, _, _ = plan_offsets(rows)
    copy_a = pltpu.make_async_copy(tiles_a, held_a, sems.at[0])
    copy_b = pltpu.make_async_copy(tiles_b, held_b, sems.at[1])
    copy_a.start()
    copy_b.start()

    def clear(i, carry):
        acc[i] = jnp.zeros_like(acc[i])
        return carry

    lax.fori_loop(0, acc.shape[0], clear, 0)
    for s, (copy, tiles, cot) in enumerate(((copy_a, held_a, cot_a), (copy_b, held_b, cot_b))):
        copy.wait()

        def block(b, carry, s=s, tiles=tiles, cot=cot):
            turned = cot[pl.ds(pl.multiple_of(b * blk, blk), blk), :].T
            base = (s * rows + b) * STRIDE

            def one(i, carry):
                for j in range(UNROLL // 2):
                    at = base + i * UNROLL + 2 * j
                    one_tile, two_tile = lists[2 * span + at], lists[2 * span + at + 1]
                    right = jnp.concatenate([tiles[one_tile], tiles[two_tile]], axis=1)
                    term = jnp.dot(turned, right, preferred_element_type=jnp.float32)
                    one_slot, two_slot = lists[3 * span + at], lists[3 * span + at + 1]
                    acc[one_slot] = acc[one_slot] + term[:, :blk]
                    acc[two_slot] = acc[two_slot] + term[:, blk:]
                return carry

            return lax.fori_loop(0, lists[counts + 2 * rows + s * rows + b], one, carry)

        lax.fori_loop(0, rows, block, 0)
    size = outs[0].shape[0]

    def store(i, carry):
        for r, out in enumerate(outs):
            out[i] = acc[r * size + i].astype(out.dtype)
        return carry

    lax.fori_loop(0, size, store, 0)


def transposed_terms(lists, tiles_a, tiles_b, cot_a, cot_b, total):
    blk = tiles_a.shape[1]
    width = cot_a.shape[1]
    shape = jax.ShapeDtypeStruct((total // NX, width, blk), jnp.bfloat16)
    smem = pl.BlockSpec(memory_space=pltpu.SMEM)
    vmem = pl.BlockSpec(memory_space=pltpu.VMEM)
    free = pl.BlockSpec(memory_space=pltpu.HBM)
    return pl.pallas_call(
        transposed_kernel,
        out_shape=[shape] * NX,
        in_specs=[smem, free, free, vmem, vmem],
        out_specs=[vmem] * NX,
        scratch_shapes=[
            pltpu.VMEM((total + 1, width, blk), jnp.float32),
            pltpu.VMEM(tiles_a.shape, tiles_a.dtype),
            pltpu.VMEM(tiles_b.shape, tiles_b.dtype),
            pltpu.SemaphoreType.DMA((2,)),
        ],
        compiler_params=pltpu.CompilerParams(vmem_limit_bytes=32 * 1024 * 1024),
        name="transposed_terms",
    )(lists, in_hbm(tiles_a), in_hbm(tiles_b), cot_a, cot_b)


def early_call(lists, tiles_a, tiles_b, pieces, total, rows):
    blk = tiles_a.shape[1]
    width = pieces[0][2].shape[2]
    n = len(pieces)
    span, counts, _, _ = plan_offsets(rows)

    def kernel(lists, tiles_a, tiles_b, *rest):
        parts, (out_a, out_b, held, held_a, held_b, sems) = rest[:n], rest[n:]
        copies = [
            pltpu.make_async_copy(part.at[pl.ds(0, count)], held.at[pl.ds(at, count)], sems.at[i])
            for i, (part, (at, count, _)) in enumerate(zip(parts, pieces))
        ]
        copy_a = pltpu.make_async_copy(tiles_a, held_a, sems.at[n])
        copy_b = pltpu.make_async_copy(tiles_b, held_b, sems.at[n + 1])
        for copy in copies:
            copy.start()
        copy_b.start()
        copy_a.start()
        held[total] = jnp.zeros_like(held[total])
        for copy in copies:
            copy.wait()
        for s, copy, tiles, out in ((1, copy_b, held_b, out_b), (0, copy_a, held_a, out_a)):
            copy.wait()

            def block(b, carry, s=s, tiles=tiles, out=out):
                base = (s * rows + b) * STRIDE

                def one(i, summed):
                    for j in range(UNROLL // 2):
                        at = base + i * UNROLL + 2 * j
                        left = jnp.concatenate([tiles[lists[at]], tiles[lists[at + 1]]], axis=1)
                        one_slot, two_slot = lists[span + at], lists[span + at + 1]
                        right = jnp.concatenate([held[one_slot], held[two_slot]], axis=0)
                        summed = summed + jnp.dot(left, right, preferred_element_type=jnp.float32)
                    return summed

                zero = jnp.zeros((blk, width), jnp.float32)
                out[b] = lax.fori_loop(0, lists[counts + s * rows + b], one, zero)
                return carry

            lax.fori_loop(0, rows, block, 0)

    shape = jax.ShapeDtypeStruct((rows, blk, width), jnp.float32)
    smem = pl.BlockSpec(memory_space=pltpu.SMEM)
    vmem = pl.BlockSpec(memory_space=pltpu.VMEM)
    free = pl.BlockSpec(memory_space=pltpu.HBM)
    return pl.pallas_call(
        kernel,
        out_shape=[shape, shape],
        in_specs=[smem] + [free] * (n + 2),
        out_specs=[vmem, vmem],
        scratch_shapes=[
            pltpu.VMEM((total + 1, blk, width), jnp.bfloat16),
            pltpu.VMEM(tiles_a.shape, tiles_a.dtype),
            pltpu.VMEM(tiles_b.shape, tiles_b.dtype),
            pltpu.SemaphoreType.DMA((n + 2,)),
        ],
        compiler_params=pltpu.CompilerParams(vmem_limit_bytes=24 * 1024 * 1024),
        name="early",
    )(lists, in_hbm(tiles_a), in_hbm(tiles_b), *[in_hbm(part) for _, _, part in pieces])


def late_call(lists, tiles_a, tiles_b, last, early):
    rows, blk, width = early[0].shape
    n = len(last)
    zero = sum(count for _, count, _ in last)
    _, _, late, _ = plan_offsets(rows)

    def kernel(lists, tiles_a, tiles_b, early_a, early_b, *rest):
        parts, (out_a, out_b, held, got, sems) = rest[:n], rest[n:]
        copies = [
            pltpu.make_async_copy(part.at[pl.ds(0, count)], held.at[pl.ds(at, count)], sems.at[i])
            for i, (part, (at, count, _)) in enumerate(zip(parts, last))
        ]
        for s, tiles in ((0, tiles_a), (1, tiles_b)):
            for j in range(LATE):
                at = s * LATE + j
                tile = lists[late + 2 * LATE * s + j]
                copies.append(pltpu.make_async_copy(tiles.at[tile], got.at[at], sems.at[n + at]))
        for copy in copies:
            copy.start()
        held[zero] = jnp.zeros_like(held[zero])
        out_a[...] = early_a[...]
        out_b[...] = early_b[...]
        for copy in copies:
            copy.wait()
        for s, out in ((0, out_a), (1, out_b)):

            def some(i, carry, s=s, out=out):
                for j in range(2):
                    k = i * 2 + j
                    at = late + 2 * LATE * s + k
                    term = jnp.dot(got[s * LATE + k], held[lists[at + 4 * LATE]], preferred_element_type=jnp.float32)
                    row = lists[at + 8 * LATE]
                    out[row] = out[row] + term
                return carry

            lax.fori_loop(0, LATE // 2, some, 0)

    shape = jax.ShapeDtypeStruct((rows, blk, width), jnp.float32)
    smem = pl.BlockSpec(memory_space=pltpu.SMEM)
    vmem = pl.BlockSpec(memory_space=pltpu.VMEM)
    free = pl.BlockSpec(memory_space=pl.ANY)
    tiled = pl.BlockSpec(memory_space=pltpu.HBM)
    return pl.pallas_call(
        kernel,
        out_shape=[shape, shape],
        in_specs=[smem, tiled, tiled, vmem, vmem] + [free] * n,
        out_specs=[vmem, vmem],
        scratch_shapes=[
            pltpu.VMEM((zero + 1, blk, width), jnp.bfloat16),
            pltpu.VMEM((2 * LATE, blk, blk), tiles_a.dtype),
            pltpu.SemaphoreType.DMA((n + 2 * LATE,)),
        ],
        compiler_params=pltpu.CompilerParams(vmem_limit_bytes=8 * 1024 * 1024),
        name="late",
    )(lists, in_hbm(tiles_a), in_hbm(tiles_b), *early, *[part for _, _, part in last])


def mixing_kernel(place, p0, p1, p2, p3, w_in, w_out, z_out, own_out, mixed_out):
    y = place[3]
    nodes, width = p0.shape
    blk = mixed_out.shape[1]

    def block(b, carry):
        at = pl.ds(pl.multiple_of(b * blk, blk), blk)
        z = None
        for r, part in enumerate((p0, p1, p2, p3)):
            row = pl.multiple_of(((y + r) & (NY - 1)) * width, width)
            term = jnp.dot(part[at, :], w_in[pl.ds(row, width), :], preferred_element_type=jnp.float32)
            z = term if z is None else z + term
        z_out[at, :] = z
        hidden = (z * jax.nn.sigmoid(z)).astype(jnp.bfloat16)
        mixed_out[b] = jnp.dot(hidden, w_out[...], preferred_element_type=jnp.float32).astype(jnp.bfloat16)
        own = z_out[at, pl.ds(pl.multiple_of(y * width, width), width)]
        own_out[at, :] = (own * jax.nn.sigmoid(own)).astype(jnp.bfloat16)
        return carry

    lax.fori_loop(0, nodes // blk, block, 0)


def mixing_call(place, parts, w_in, w_out, nb):
    nodes, width = parts[0].shape
    full = w_in.shape[0]
    smem = pl.BlockSpec(memory_space=pltpu.SMEM)
    vmem = pl.BlockSpec(memory_space=pltpu.VMEM)
    return pl.pallas_call(
        mixing_kernel,
        out_shape=[
            jax.ShapeDtypeStruct((nodes, full), jnp.float32),
            jax.ShapeDtypeStruct((nodes, width), jnp.bfloat16),
            jax.ShapeDtypeStruct((nb, nodes // nb, width), jnp.bfloat16),
        ],
        in_specs=[smem] + [vmem] * (NY + 2),
        out_specs=[vmem] * 3,
        compiler_params=pltpu.CompilerParams(vmem_limit_bytes=16 * 1024 * 1024),
        name="mixing",
    )(place, *parts, w_in, w_out)


def grads_kernel(place, z_all, prop, own, q0, q1, q2, q3, w_two, keep, give, both, *, factor):
    y = place[3]
    nodes, width = prop.shape
    blk = 128 if nodes % 128 == 0 else nodes
    down = (((0,), (0,)), ((), ()))
    across = (((1,), (1,)), ((), ()))
    both[...] = jnp.zeros_like(both)

    def block(b, carry):
        at = pl.ds(pl.multiple_of(b * blk, blk), blk)
        hidden_grad = None
        for r, part in enumerate((q0, q1, q2, q3)):
            col = pl.multiple_of(((y + r) & (NY - 1)) * width, width)
            term = lax.dot_general(part[at, :], w_two[:, pl.ds(col, width)], across, preferred_element_type=jnp.float32)
            hidden_grad = term if hidden_grad is None else hidden_grad + term
            term = lax.dot_general(own[at, :], part[at, :], down, preferred_element_type=jnp.float32)
            both[1, :, pl.ds(col, width)] = both[1, :, pl.ds(col, width)] + term * factor
        z = z_all[at, :]
        sigma = jax.nn.sigmoid(z)
        grad_z = (hidden_grad * sigma * (1.0 + z * (1.0 - sigma))).astype(jnp.bfloat16)
        term = lax.dot_general(prop[at, :], grad_z, down, preferred_element_type=jnp.float32)
        both[0] = both[0] + term * factor
        return carry

    lax.fori_loop(0, nodes // blk, block, 0)
    mine = place[2]
    for r in range(NY):
        cols = slice(r * width, (r + 1) * width)
        rows = slice(r * width, (r + 1) * width)
        keep[rows, :] = both[mine, :, cols]
        give[rows, :] = both[1 - mine, :, cols]


def grads_call(place, z_all, prop, own, parts, w_two, factor):
    width = prop.shape[1]
    full = w_two.shape[0]
    smem = pl.BlockSpec(memory_space=pltpu.SMEM)
    vmem = pl.BlockSpec(memory_space=pltpu.VMEM)
    return pl.pallas_call(
        functools.partial(grads_kernel, factor=factor),
        out_shape=[jax.ShapeDtypeStruct((full, width), jnp.float32)] * 2,
        in_specs=[smem] + [vmem] * (NY + 4),
        out_specs=[vmem] * 2,
        scratch_shapes=[pltpu.VMEM((2, width, full), jnp.float32)],
        compiler_params=pltpu.CompilerParams(vmem_limit_bytes=16 * 1024 * 1024),
        name="grads",
    )(place, z_all, prop, own, *parts, w_two)


def step(node_feats, weight_one, weight_two, adj_tiles, tile_owner, tile_local, cotangent):
    nb, per, blk, _ = adj_tiles.shape
    nodes, width = node_feats.shape
    full = weight_one.shape[0]
    node_count = NX * NZ * NC
    index = lax.axis_index("nodes")
    y = lax.axis_index("feat")
    place = jnp.stack([index // (NZ * NC), (index // NC) % NZ, index % NC, y]).astype(jnp.int32)
    bf = jnp.bfloat16
    total = NX * NZ * nb

    tiles = adj_tiles.reshape(nb * per, blk, blk)
    column = (tile_owner * nb + tile_local)[:, 0]
    column_other = send(column, dc=1)
    tiles_other = send(tiles, dc=1)
    cot_other = send(cotangent, dc=1)
    lists = plan_call(place, column, column_other, nb, per)

    def spread(features):
        near, last = gather_plane(features)
        early = early_call(lists, tiles, tiles_other, near, total, nb)
        mine, theirs = late_call(lists, tiles, tiles_other, last, early)
        return (mine + send(theirs, dc=1)).reshape(nodes, width).astype(bf)

    terms = transposed_terms(lists, tiles, tiles_other, cotangent, cot_other, total)
    turned = jnp.swapaxes(reduce_plane(terms, nb), 1, 2).reshape(nodes, width).astype(bf)

    weight_out = lax.dynamic_slice_in_dim(weight_two, y * width, width, 1)
    prop_one = spread(node_feats.reshape(nb, blk, width))
    prop_parts = gather_y(prop_one)
    z_one, hidden_own, mixed = mixing_call(place, prop_parts, weight_one, weight_out, nb)

    turned_parts = gather_y(turned)
    factor = 1.0 / math.sqrt(nodes * node_count)
    both = grads_call(place, z_one, prop_one, hidden_own, turned_parts, weight_two, factor)
    part = halve(both, index)
    layer_output = spread(mixed)
    summed = double(part, index).reshape(2, NY, width, width)
    summed = jnp.swapaxes(summed, 1, 2).reshape(2, width, full)
    return (layer_output, summed[0], summed[1])


def solution(mesh):
    placed = (
        P("nodes", "feat"),
        P(),
        P(),
        P("nodes", None, None, None),
        P("nodes", None),
        P("nodes", None),
        P("nodes", "feat"),
    )
    return jax.shard_map(
        step,
        mesh=mesh,
        in_specs=placed,
        out_specs=(P("nodes", "feat"), P("feat", None), P("feat", None)),
        check_vma=False,
    )
```

```python
import functools
import math

import jax
import jax.numpy as jnp
from jax import lax
from jax.experimental import pallas as pl
from jax.experimental.pallas import tpu as pltpu
from jax.sharding import PartitionSpec as P


NX, NZ, NC, NY = 4, 8, 2, 4


STRIDE = 32
UNROLL = 6
LATE = 8


def node_pairs(dx, dz, dc):
    pairs = []
    for x in range(NX):
        for z in range(NZ):
            for c in range(NC):
                there = (((x + dx) % NX) * NZ + (z + dz) % NZ) * NC + (c + dc) % NC
                pairs.append(((x * NZ + z) * NC + c, there))
    return pairs


def xor_pairs(bit):
    return [(i, i ^ bit) for i in range(NX * NZ * NC)]


def in_hbm(value):
    return pltpu.with_memory_space_constraint(value, pltpu.HBM)


def send(value, dx=0, dz=0, dc=0):
    return lax.ppermute(value, "nodes", node_pairs(dx, dz, dc))


def gather_y(value):
    pairs = [[(y, (y - r) % NY) for y in range(NY)] for r in range(NY)]
    return [value] + [lax.ppermute(value, "feat", pairs[r]) for r in range(1, NY)]


def ring_z(block):
    half = block.shape[0] // 2
    low, high = [block], [block]
    for _ in range(1, 4):
        low.append(send(low[-1], dz=1))
        high.append(send(high[-1], dz=-1))
    first = send(low[3][:half], dz=1)
    second = send(high[3][half:], dz=-1)
    return [block, high[1], high[2], high[3], (first, second), low[3], low[2], low[1]]


def gather_plane(own):
    nb = own.shape[0]
    beside = [send(own, dx=-r) for r in (1, 2, 3)]
    near, last = [], []
    for r, entry in enumerate(ring_z(join_call([own] + beside))):
        if r == NZ // 2:
            half = entry[0].shape[0]
            last = [(0, half, entry[0]), (half, half, entry[1])]
        else:
            near.append((r * NX * nb, NX * nb, entry))
    return near, last


def join_call(parts):
    size, blk, width = parts[0].shape
    n = len(parts)

    def kernel(*refs):
        for i in range(n):
            refs[n][i * size:(i + 1) * size] = refs[i][...]

    vmem = pl.BlockSpec(memory_space=pltpu.VMEM)
    return pl.pallas_call(
        kernel,
        out_shape=jax.ShapeDtypeStruct((n * size, blk, width), parts[0].dtype),
        in_specs=[vmem] * n,
        out_specs=vmem,
        compiler_params=pltpu.CompilerParams(vmem_limit_bytes=4 * 1024 * 1024),
        name="join",
    )(*parts)


def fold_kernel(p1, p3, up_far, down_far, up, down):
    half = up_far.shape[0]
    f32 = jnp.float32

    def one(i, carry):
        up[i] = (p1[i].astype(f32) + up_far[i].astype(f32)).astype(up.dtype)
        up[half + i] = p1[half + i]
        down[i] = p3[i]
        down[half + i] = (p3[half + i].astype(f32) + down_far[i].astype(f32)).astype(down.dtype)
        return carry

    lax.fori_loop(0, half, one, 0)


def fold_call(p1, p3, up_far, down_far):
    vmem = pl.BlockSpec(memory_space=pltpu.VMEM)
    return pl.pallas_call(
        fold_kernel,
        out_shape=[jax.ShapeDtypeStruct(p1.shape, p1.dtype)] * 2,
        in_specs=[vmem] * 4,
        out_specs=[vmem] * 2,
        compiler_params=pltpu.CompilerParams(vmem_limit_bytes=8 * 1024 * 1024),
        name="fold",
    )(p1, p3, up_far, down_far)


def sum_kernel(p0, up, down, keep, give):
    half = keep.shape[0]
    f32 = jnp.float32

    def one(i, carry):
        keep[i] = p0[i].astype(f32) + up[i].astype(f32) + down[i].astype(f32)
        far = half + i
        give[i] = (p0[far].astype(f32) + up[far].astype(f32) + down[far].astype(f32)).astype(give.dtype)
        return carry

    lax.fori_loop(0, half, one, 0)


def sum_call(p0, up, down):
    vmem = pl.BlockSpec(memory_space=pltpu.VMEM)
    size, width, blk = p0.shape
    return pl.pallas_call(
        sum_kernel,
        out_shape=[
            jax.ShapeDtypeStruct((size // 2, width, blk), jnp.float32),
            jax.ShapeDtypeStruct((size // 2, width, blk), p0.dtype),
        ],
        in_specs=[vmem] * 3,
        out_specs=[vmem] * 2,
        compiler_params=pltpu.CompilerParams(vmem_limit_bytes=8 * 1024 * 1024),
        name="sum",
    )(p0, up, down)


def reduce_plane(parts, nb):
    f32, bf = jnp.float32, jnp.bfloat16
    half = NZ * nb // 2
    far = parts[2]
    up_far = send(far[:half], dx=1)
    down_far = send(far[half:], dx=-1)
    up, down = fold_call(parts[1], parts[3], up_far, down_far)
    own, give = sum_call(parts[0], send(up, dx=1), send(down, dx=-1))
    own = own + lax.ppermute(give, "nodes", xor_pairs(NC)).astype(f32)
    for bit in (2, 4):
        half = own.shape[0] // 2
        give = own[half:].astype(bf)
        own = own[:half] + lax.ppermute(give, "nodes", xor_pairs(bit * NC)).astype(f32)
    return own


def halve(value, index):
    value, give = value
    value = value + lax.ppermute(give, "nodes", xor_pairs(1))
    for bit in (16,):
        half = value.shape[0] // 2
        upper = (index & bit) != 0
        mine = jnp.where(upper, value[half:], value[:half])
        give = jnp.where(upper, value[:half], value[half:])
        value = mine + lax.ppermute(give, "nodes", xor_pairs(bit))
    for bit in (32, 2, 4, 8):
        value = value + lax.ppermute(value, "nodes", xor_pairs(bit))
    return value


def double(value, index):
    for bit in (16, 1):
        upper = (index & bit) != 0
        other = lax.ppermute(value, "nodes", xor_pairs(bit))
        value = jnp.concatenate([jnp.where(upper, other, value), jnp.where(upper, value, other)], axis=0)
    return value


def plan_offsets(nb):
    span = 2 * nb * STRIDE
    counts = 4 * span
    late = counts + 4 * nb
    return span, counts, late, late + 8 * LATE * 3


def plan_kernel(place, col_a, col_b, lists, *, nb, per):
    bits = nb.bit_length() - 1
    x, z, c = place[0], place[1], place[2]
    total = NX * NZ * nb
    span, counts, late, _ = plan_offsets(nb)
    for j in range(4 * LATE):
        lists[late + j] = 0
        lists[late + 4 * LATE + j] = NX * nb
        lists[late + 8 * LATE + j] = 0
    for s, cols in enumerate((col_a, col_b)):

        def block(b, behind, cols=cols, s=s):
            base = (s * nb + b) * STRIDE

            def one(k, carry):
                early, every, behind = carry
                column = cols[b * per + k]
                local = column & (nb - 1)
                owner = column >> bits
                rx = ((owner >> 4) - x) & (NX - 1)
                zo = (owner >> 1) & (NZ - 1)
                rz = (zo - z) & (NZ - 1)
                rel = zo ^ z
                rank = ((rel & 1) << 2) | (rel & 2) | (rel >> 2)
                mine = jnp.where((owner & 1) == c, 1, 0)
                far = jnp.where(rz == NZ // 2, mine, 0)
                lists[base + early] = b * per + k
                lists[span + base + early] = (rz * NX + rx) * nb + local
                lists[2 * span + base + every] = b * per + k
                lists[3 * span + base + every] = (rx * NZ + rank) * nb + local
                at = late + 2 * LATE * s + behind
                lists[at] = b * per + k
                lists[at + 4 * LATE] = rx * nb + local
                lists[at + 8 * LATE] = b
                return early + mine - far, every + mine, behind + far

            early, every, behind = lax.fori_loop(0, per, one, (0, 0, behind))
            lists[counts + s * nb + b] = (early + UNROLL - 1) // UNROLL
            lists[counts + 2 * nb + s * nb + b] = (every + UNROLL - 1) // UNROLL
            for j in range(UNROLL):
                lists[base + early + j] = 0
                lists[span + base + early + j] = total
                lists[2 * span + base + every + j] = 0
                lists[3 * span + base + every + j] = total
            return behind

        behind = lax.fori_loop(0, nb, block, 0)
        at = late + 2 * LATE * s + behind
        lists[at] = 0
        lists[at + 4 * LATE] = NX * nb
        lists[at + 8 * LATE] = 0


def plan_call(place, col_a, col_b, nb, per):
    smem = pl.BlockSpec(memory_space=pltpu.SMEM)
    return pl.pallas_call(
        functools.partial(plan_kernel, nb=nb, per=per),
        out_shape=jax.ShapeDtypeStruct((plan_offsets(nb)[3],), jnp.int32),
        in_specs=[smem] * 3,
        out_specs=smem,
        name="plan",
    )(place, col_a, col_b)


def transposed_kernel(lists, tiles_a, tiles_b, cot_a, cot_b, *rest):
    outs, (acc, held_a, held_b, sems) = rest[:NX], rest[NX:]
    blk = held_a.shape[1]
    rows = cot_a.shape[0] // blk
    span, counts, _, _ = plan_offsets(rows)
    copy_a = pltpu.make_async_copy(tiles_a, held_a, sems.at[0])
    copy_b = pltpu.make_async_copy(tiles_b, held_b, sems.at[1])
    copy_a.start()
    copy_b.start()

    def clear(i, carry):
        acc[i] = jnp.zeros_like(acc[i])
        return carry

    lax.fori_loop(0, acc.shape[0], clear, 0)
    for s, (copy, tiles, cot) in enumerate(((copy_a, held_a, cot_a), (copy_b, held_b, cot_b))):
        copy.wait()

        def block(b, carry, s=s, tiles=tiles, cot=cot):
            turned = cot[pl.ds(pl.multiple_of(b * blk, blk), blk), :].T
            base = (s * rows + b) * STRIDE

            def one(i, carry):
                for j in range(UNROLL // 2):
                    at = base + i * UNROLL + 2 * j
                    one_tile, two_tile = lists[2 * span + at], lists[2 * span + at + 1]
                    right = jnp.concatenate([tiles[one_tile], tiles[two_tile]], axis=1)
                    term = jnp.dot(turned, right, preferred_element_type=jnp.float32)
                    one_slot, two_slot = lists[3 * span + at], lists[3 * span + at + 1]
                    acc[one_slot] = acc[one_slot] + term[:, :blk]
                    acc[two_slot] = acc[two_slot] + term[:, blk:]
                return carry

            return lax.fori_loop(0, lists[counts + 2 * rows + s * rows + b], one, carry)

        lax.fori_loop(0, rows, block, 0)
    size = outs[0].shape[0]

    def store(i, carry):
        for r, out in enumerate(outs):
            out[i] = acc[r * size + i].astype(out.dtype)
        return carry

    lax.fori_loop(0, size, store, 0)


def transposed_terms(lists, tiles_a, tiles_b, cot_a, cot_b, total):
    blk = tiles_a.shape[1]
    width = cot_a.shape[1]
    shape = jax.ShapeDtypeStruct((total // NX, width, blk), jnp.bfloat16)
    smem = pl.BlockSpec(memory_space=pltpu.SMEM)
    vmem = pl.BlockSpec(memory_space=pltpu.VMEM)
    free = pl.BlockSpec(memory_space=pltpu.HBM)
    return pl.pallas_call(
        transposed_kernel,
        out_shape=[shape] * NX,
        in_specs=[smem, free, free, vmem, vmem],
        out_specs=[vmem] * NX,
        scratch_shapes=[
            pltpu.VMEM((total + 1, width, blk), jnp.float32),
            pltpu.VMEM(tiles_a.shape, tiles_a.dtype),
            pltpu.VMEM(tiles_b.shape, tiles_b.dtype),
            pltpu.SemaphoreType.DMA((2,)),
        ],
        compiler_params=pltpu.CompilerParams(vmem_limit_bytes=32 * 1024 * 1024),
        name="transposed_terms",
    )(lists, in_hbm(tiles_a), in_hbm(tiles_b), cot_a, cot_b)


def early_call(lists, tiles_a, tiles_b, pieces, total, rows):
    blk = tiles_a.shape[1]
    width = pieces[0][2].shape[2]
    n = len(pieces)
    span, counts, _, _ = plan_offsets(rows)

    def kernel(lists, tiles_a, tiles_b, *rest):
        parts, (out_a, out_b, held, held_a, held_b, sems) = rest[:n], rest[n:]
        copies = [
            pltpu.make_async_copy(part.at[pl.ds(0, count)], held.at[pl.ds(at, count)], sems.at[i])
            for i, (part, (at, count, _)) in enumerate(zip(parts, pieces))
        ]
        copy_a = pltpu.make_async_copy(tiles_a, held_a, sems.at[n])
        copy_b = pltpu.make_async_copy(tiles_b, held_b, sems.at[n + 1])
        for copy in copies:
            copy.start()
        copy_b.start()
        copy_a.start()
        held[total] = jnp.zeros_like(held[total])
        for copy in copies:
            copy.wait()
        for s, copy, tiles, out in ((1, copy_b, held_b, out_b), (0, copy_a, held_a, out_a)):
            copy.wait()

            def block(b, carry, s=s, tiles=tiles, out=out):
                base = (s * rows + b) * STRIDE

                def one(i, summed):
                    for j in range(UNROLL // 2):
                        at = base + i * UNROLL + 2 * j
                        left = jnp.concatenate([tiles[lists[at]], tiles[lists[at + 1]]], axis=1)
                        one_slot, two_slot = lists[span + at], lists[span + at + 1]
                        right = jnp.concatenate([held[one_slot], held[two_slot]], axis=0)
                        summed = summed + jnp.dot(left, right, preferred_element_type=jnp.float32)
                    return summed

                zero = jnp.zeros((blk, width), jnp.float32)
                out[b] = lax.fori_loop(0, lists[counts + s * rows + b], one, zero)
                return carry

            lax.fori_loop(0, rows, block, 0)

    shape = jax.ShapeDtypeStruct((rows, blk, width), jnp.float32)
    smem = pl.BlockSpec(memory_space=pltpu.SMEM)
    vmem = pl.BlockSpec(memory_space=pltpu.VMEM)
    free = pl.BlockSpec(memory_space=pltpu.HBM)
    return pl.pallas_call(
        kernel,
        out_shape=[shape, shape],
        in_specs=[smem] + [free] * (n + 2),
        out_specs=[vmem, vmem],
        scratch_shapes=[
            pltpu.VMEM((total + 1, blk, width), jnp.bfloat16),
            pltpu.VMEM(tiles_a.shape, tiles_a.dtype),
            pltpu.VMEM(tiles_b.shape, tiles_b.dtype),
            pltpu.SemaphoreType.DMA((n + 2,)),
        ],
        compiler_params=pltpu.CompilerParams(vmem_limit_bytes=24 * 1024 * 1024),
        name="early",
    )(lists, in_hbm(tiles_a), in_hbm(tiles_b), *[in_hbm(part) for _, _, part in pieces])


def late_call(lists, tiles_a, tiles_b, last, early):
    rows, blk, width = early[0].shape
    n = len(last)
    zero = sum(count for _, count, _ in last)
    _, _, late, _ = plan_offsets(rows)

    def kernel(lists, tiles_a, tiles_b, early_a, early_b, *rest):
        parts, (out_a, out_b, held, got, sems) = rest[:n], rest[n:]
        copies = [
            pltpu.make_async_copy(part.at[pl.ds(0, count)], held.at[pl.ds(at, count)], sems.at[i])
            for i, (part, (at, count, _)) in enumerate(zip(parts, last))
        ]
        for s, tiles in ((0, tiles_a), (1, tiles_b)):
            for j in range(LATE):
                at = s * LATE + j
                tile = lists[late + 2 * LATE * s + j]
                copies.append(pltpu.make_async_copy(tiles.at[tile], got.at[at], sems.at[n + at]))
        for copy in copies:
            copy.start()
        held[zero] = jnp.zeros_like(held[zero])
        out_a[...] = early_a[...]
        out_b[...] = early_b[...]
        for copy in copies:
            copy.wait()
        for s, out in ((0, out_a), (1, out_b)):

            def some(i, carry, s=s, out=out):
                for j in range(LATE // 2):
                    k = i * (LATE // 2) + j
                    at = late + 2 * LATE * s + k
                    term = jnp.dot(got[s * LATE + k], held[lists[at + 4 * LATE]], preferred_element_type=jnp.float32)
                    row = lists[at + 8 * LATE]
                    out[row] = out[row] + term
                return carry

            lax.fori_loop(0, 2, some, 0)

    shape = jax.ShapeDtypeStruct((rows, blk, width), jnp.float32)
    smem = pl.BlockSpec(memory_space=pltpu.SMEM)
    vmem = pl.BlockSpec(memory_space=pltpu.VMEM)
    free = pl.BlockSpec(memory_space=pl.ANY)
    tiled = pl.BlockSpec(memory_space=pltpu.HBM)
    return pl.pallas_call(
        kernel,
        out_shape=[shape, shape],
        in_specs=[smem, tiled, tiled, vmem, vmem] + [free] * n,
        out_specs=[vmem, vmem],
        scratch_shapes=[
            pltpu.VMEM((zero + 1, blk, width), jnp.bfloat16),
            pltpu.VMEM((2 * LATE, blk, blk), tiles_a.dtype),
            pltpu.SemaphoreType.DMA((n + 2 * LATE,)),
        ],
        compiler_params=pltpu.CompilerParams(vmem_limit_bytes=8 * 1024 * 1024),
        name="late",
    )(lists, in_hbm(tiles_a), in_hbm(tiles_b), *early, *[part for _, _, part in last])


def mixing_kernel(place, p0, p1, p2, p3, w_in, w_out, z_out, own_out, mixed_out):
    y = place[3]
    nodes, width = p0.shape
    blk = mixed_out.shape[1]

    def block(b, carry):
        at = pl.ds(pl.multiple_of(b * blk, blk), blk)
        z = None
        for r, part in enumerate((p0, p1, p2, p3)):
            row = pl.multiple_of(((y + r) & (NY - 1)) * width, width)
            term = jnp.dot(part[at, :], w_in[pl.ds(row, width), :], preferred_element_type=jnp.float32)
            z = term if z is None else z + term
        z_out[at, :] = z
        hidden = (z * jax.nn.sigmoid(z)).astype(jnp.bfloat16)
        mixed_out[b] = jnp.dot(hidden, w_out[...], preferred_element_type=jnp.float32).astype(jnp.bfloat16)
        own = z_out[at, pl.ds(pl.multiple_of(y * width, width), width)]
        own_out[at, :] = (own * jax.nn.sigmoid(own)).astype(jnp.bfloat16)
        return carry

    lax.fori_loop(0, nodes // blk, block, 0)


def mixing_call(place, parts, w_in, w_out, nb):
    nodes, width = parts[0].shape
    full = w_in.shape[0]
    smem = pl.BlockSpec(memory_space=pltpu.SMEM)
    vmem = pl.BlockSpec(memory_space=pltpu.VMEM)
    return pl.pallas_call(
        mixing_kernel,
        out_shape=[
            jax.ShapeDtypeStruct((nodes, full), jnp.float32),
            jax.ShapeDtypeStruct((nodes, width), jnp.bfloat16),
            jax.ShapeDtypeStruct((nb, nodes // nb, width), jnp.bfloat16),
        ],
        in_specs=[smem] + [vmem] * (NY + 2),
        out_specs=[vmem] * 3,
        compiler_params=pltpu.CompilerParams(vmem_limit_bytes=16 * 1024 * 1024),
        name="mixing",
    )(place, *parts, w_in, w_out)


def grads_kernel(place, z_all, prop, own, q0, q1, q2, q3, w_two, keep, give, both, *, factor):
    y = place[3]
    nodes, width = prop.shape
    blk = 128 if nodes % 128 == 0 else nodes
    down = (((0,), (0,)), ((), ()))
    across = (((1,), (1,)), ((), ()))
    both[...] = jnp.zeros_like(both)

    def block(b, carry):
        at = pl.ds(pl.multiple_of(b * blk, blk), blk)
        hidden_grad = None
        for r, part in enumerate((q0, q1, q2, q3)):
            col = pl.multiple_of(((y + r) & (NY - 1)) * width, width)
            term = lax.dot_general(part[at, :], w_two[:, pl.ds(col, width)], across, preferred_element_type=jnp.float32)
            hidden_grad = term if hidden_grad is None else hidden_grad + term
            term = lax.dot_general(own[at, :], part[at, :], down, preferred_element_type=jnp.float32)
            both[1, :, pl.ds(col, width)] = both[1, :, pl.ds(col, width)] + term * factor
        z = z_all[at, :]
        sigma = jax.nn.sigmoid(z)
        grad_z = (hidden_grad * sigma * (1.0 + z * (1.0 - sigma))).astype(jnp.bfloat16)
        term = lax.dot_general(prop[at, :], grad_z, down, preferred_element_type=jnp.float32)
        both[0] = both[0] + term * factor
        return carry

    lax.fori_loop(0, nodes // blk, block, 0)
    mine = place[2]
    for r in range(NY):
        cols = slice(r * width, (r + 1) * width)
        rows = slice(r * width, (r + 1) * width)
        keep[rows, :] = both[mine, :, cols]
        give[rows, :] = both[1 - mine, :, cols]


def grads_call(place, z_all, prop, own, parts, w_two, factor):
    width = prop.shape[1]
    full = w_two.shape[0]
    smem = pl.BlockSpec(memory_space=pltpu.SMEM)
    vmem = pl.BlockSpec(memory_space=pltpu.VMEM)
    return pl.pallas_call(
        functools.partial(grads_kernel, factor=factor),
        out_shape=[jax.ShapeDtypeStruct((full, width), jnp.float32)] * 2,
        in_specs=[smem] + [vmem] * (NY + 4),
        out_specs=[vmem] * 2,
        scratch_shapes=[pltpu.VMEM((2, width, full), jnp.float32)],
        compiler_params=pltpu.CompilerParams(vmem_limit_bytes=16 * 1024 * 1024),
        name="grads",
    )(place, z_all, prop, own, *parts, w_two)


def step(node_feats, weight_one, weight_two, adj_tiles, tile_owner, tile_local, cotangent):
    nb, per, blk, _ = adj_tiles.shape
    nodes, width = node_feats.shape
    full = weight_one.shape[0]
    node_count = NX * NZ * NC
    index = lax.axis_index("nodes")
    y = lax.axis_index("feat")
    place = jnp.stack([index // (NZ * NC), (index // NC) % NZ, index % NC, y]).astype(jnp.int32)
    bf = jnp.bfloat16
    total = NX * NZ * nb

    tiles = adj_tiles.reshape(nb * per, blk, blk)
    column = (tile_owner * nb + tile_local)[:, 0]
    column_other = send(column, dc=1)
    tiles_other = send(tiles, dc=1)
    cot_other = send(cotangent, dc=1)
    lists = plan_call(place, column, column_other, nb, per)

    def spread(features):
        near, last = gather_plane(features)
        early = early_call(lists, tiles, tiles_other, near, total, nb)
        mine, theirs = late_call(lists, tiles, tiles_other, last, early)
        return (mine + send(theirs, dc=1)).reshape(nodes, width).astype(bf)

    terms = transposed_terms(lists, tiles, tiles_other, cotangent, cot_other, total)
    turned = jnp.swapaxes(reduce_plane(terms, nb), 1, 2).reshape(nodes, width).astype(bf)

    weight_out = lax.dynamic_slice_in_dim(weight_two, y * width, width, 1)
    prop_one = spread(node_feats.reshape(nb, blk, width))
    prop_parts = gather_y(prop_one)
    z_one, hidden_own, mixed = mixing_call(place, prop_parts, weight_one, weight_out, nb)

    turned_parts = gather_y(turned)
    factor = 1.0 / math.sqrt(nodes * node_count)
    both = grads_call(place, z_one, prop_one, hidden_own, turned_parts, weight_two, factor)
    part = halve(both, index)
    layer_output = spread(mixed)
    summed = double(part, index).reshape(2, NY, width, width)
    summed = jnp.swapaxes(summed, 1, 2).reshape(2, width, full)
    return (layer_output, summed[0], summed[1])


def solution(mesh):
    placed = (
        P("nodes", "feat"),
        P(),
        P(),
        P("nodes", None, None, None),
        P("nodes", None),
        P("nodes", None),
        P("nodes", "feat"),
    )
    return jax.shard_map(
        step,
        mesh=mesh,
        in_specs=placed,
        out_specs=(P("nodes", "feat"), P("feat", None), P("feat", None)),
        check_vma=False,
    )
```
